32 devices in a mesh: sky: 4 (over z), exp: 8 (over y, x, core).
Axes of the slice: x: 2, y: 2, z: 4, core: 2. Of those that a mesh axis runs over, the one named last changes fastest.
Arguments:
- sky_model: bfloat16 [256, 4096], P('sky'), may hold values from -6 to 6
- eigen_weights: bfloat16 [8, 256, 4096], P(None, 'sky'), may hold values from -2.09375 to 2.09375
- exposures: bfloat16 [16, 256, 4096], P('exp', 'sky'), may hold values from -6 to 6
- row_taps: bfloat16 [16, 8, 41], P('exp'), may hold values from -1 to 1
- col_taps: bfloat16 [16, 8, 41], P('exp'), may hold values from -1 to 1
- offsets: int32 [16], P('exp'), may hold values from -6 to 6, as said below
- valid_blocks: int32 [16, 16], P('exp', 'sky'), may hold values 0 or 1
Outputs:
- gradient: float32 [256, 4096], P('sky', 'exp')
The draws below stay inside these ranges and needn't reach their ends.
Inputs may be any that keep to these rules, and one draw needn't show every extreme that they name: `offsets`: every offset from -6 to 6 occurs among the exposures.
All inputs are finite; a program needn't handle non-finite values. No bound on the sum of `valid_blocks` on one device may be relied on, other than what follows from the above.
Results may differ from the reference program's by a relative error of at most 0.0024.
Values may be sent and summed in bfloat16 or wider, within the bound.
A program may use at most 128 MiB of HBM per device.

```python
import jax
import jax.numpy as jnp
from jax import lax

K = 8
TAPS = 41
SHIFT = 6
BLOCK = 16
COLS = 4096
NROWS = 256
EXPOSURES = 16
NBLOCKS = 16


def draw_offsets(key, part):
    order = jax.random.permutation(key, EXPOSURES)
    return (order % (2 * SHIFT + 1) - SHIFT).astype(jnp.int32)


def place_ends(drawn, key, low, high):
    longest = drawn.shape.index(max(drawn.shape))
    spots = []
    for shift in (0, 1):
        where = [jax.random.randint(jax.random.fold_in(key, axis), (), 0, length) for axis, length in enumerate(drawn.shape)]
        where[longest] = (where[longest] + shift) % drawn.shape[longest]
        spots.append(tuple(where))
    return drawn.at[spots[0]].set(low).at[spots[1]].set(high)


def levels(key, shape, pieces, low, top_value):
    factor_of, own = 1.0, jax.random.fold_in(key, 6)
    for axis_at, blocks in pieces:
        steps = jnp.exp(jax.random.uniform(jax.random.fold_in(own, axis_at), (blocks,), jnp.float32, low / len(pieces), top_value / len(pieces)))
        factor_of = factor_of * jnp.repeat(steps, shape[axis_at] // blocks).reshape([-1 if axis == axis_at else 1 for axis in range(len(shape))])
    return factor_of


def normal_values(key, extent, scale, limit, split=(), kind=jnp.bfloat16):
    values = scale * jax.random.normal(key, extent, jnp.float32)
    if split:
        values = values * levels(key, extent, split, -0.22, 0.18)
    return jnp.clip(values, -limit, limit).astype(kind)


def setup_inputs(seed: int = 0) -> dict:
    seeds = jax.random.split(jax.random.key(seed), 8)
    sky_model = normal_values(seeds[0], (NROWS, COLS), 1.0, 6.0, ((0, 4),))
    eigen_weights = normal_values(seeds[1], (K, NROWS, COLS), 0.35, 2.09375, ((1, 4),))
    exposures = normal_values(seeds[2], (EXPOSURES, NROWS, COLS), 1.0, 6.0, ((0, 8), (1, 4)))
    row_taps = normal_values(seeds[3], (EXPOSURES, K, TAPS), TAPS ** -0.5, 1.0, ((0, 8),))
    col_taps = normal_values(seeds[4], (EXPOSURES, K, TAPS), TAPS ** -0.5, 1.0, ((0, 8),))
    offsets = draw_offsets(jax.random.fold_in(seeds[7], 71), 0)
    valid_blocks = place_ends((jax.random.randint(seeds[6], (EXPOSURES, NBLOCKS), 0, 4) < 3).astype(jnp.int32), jax.random.fold_in(seeds[6], 1), 0, 1)
    return {"sky_model": sky_model, "eigen_weights": eigen_weights, "exposures": exposures, "row_taps": row_taps, "col_taps": col_taps, "offsets": offsets, "valid_blocks": valid_blocks}


def filter_axis(field, taps, vertical):
    half = taps.shape[1] // 2
    if vertical:
        kernel = taps[:, None, :, None]
        padding = ((half, half), (0, 0))
    else:
        kernel = taps[:, None, None, :]
        padding = ((0, 0), (half, half))
    result = lax.conv_general_dilated(field[None], kernel, (1, 1), padding, dimension_numbers=("NCHW", "OIHW", "NCHW"), feature_group_count=field.shape[0], precision=lax.Precision.HIGHEST)
    return result[0]


def move_columns(field, offset):
    padded = jnp.pad(field, ((0, 0), (SHIFT, SHIFT)))
    start = (SHIFT - offset).astype(jnp.int32)
    return lax.dynamic_slice_in_dim(padded, start, field.shape[1], 1)


def reference(sky_model, eigen_weights, exposures, row_taps, col_taps, offsets, valid_blocks):
    weights32 = eigen_weights.astype(jnp.float32)
    product = (weights32 * sky_model.astype(jnp.float32)[None]).astype(jnp.bfloat16)
    product = lax.optimization_barrier(product).astype(jnp.float32)

    def one_frame(gradient, inputs):
        rtaps, ctaps, offset, mask_row, data = inputs
        rtaps = rtaps.astype(jnp.float32)
        ctaps = ctaps.astype(jnp.float32)
        blurred = filter_axis(product, ctaps, False).astype(jnp.bfloat16)
        blurred = lax.optimization_barrier(blurred).astype(jnp.float32)
        image = jnp.sum(filter_axis(blurred, rtaps, True), axis=0)
        placed = move_columns(image, offset)
        rowmask = jnp.repeat(mask_row, BLOCK).astype(jnp.float32)
        residual = (rowmask[:, None] * (placed - data.astype(jnp.float32))).astype(jnp.bfloat16)
        residual = lax.optimization_barrier(residual).astype(jnp.float32)
        moved = move_columns(residual, -offset)
        spread = filter_axis(jnp.broadcast_to(moved[None], product.shape), ctaps[:, ::-1], False).astype(jnp.bfloat16)
        spread = lax.optimization_barrier(spread).astype(jnp.float32)
        lifted = filter_axis(spread, rtaps[:, ::-1], True)
        return gradient + jnp.sum(weights32 * lifted, axis=0), None

    start = jnp.zeros(sky_model.shape, jnp.float32)
    gradient, _ = lax.scan(one_frame, start, (row_taps, col_taps, offsets, valid_blocks, exposures))
    return gradient
```

```python
import functools

import jax
import jax.numpy as jnp
from jax import lax
from jax.experimental import pallas as pl
from jax.experimental.pallas import tpu as pltpu
from jax.sharding import PartitionSpec as P

F32 = jnp.float32
BF16 = jnp.bfloat16
LANE = 128
PAD = 64
SLOT = 24
REACH = 20
CHUNK = 512


def lagged(taps, lanes, sign, start):
    width = taps.shape[1]
    lane = lax.broadcasted_iota(jnp.int32, (width, lanes), 1)
    lag = jnp.where(lane < lanes // 2, lane, lane - lanes)
    tap = lax.broadcasted_iota(jnp.int32, (width, lanes), 0)
    onehot = jnp.where(tap == sign * lag + start, 1.0, 0.0).astype(BF16)
    return jnp.dot(taps, onehot, preferred_element_type=F32)


def toeplitz(row, height, shift=0):
    full = jnp.broadcast_to(row, (height, row.shape[1]))
    return pltpu.roll(full, shift, 1, stride=1, stride_axis=0)


def forward_tables(frames, count, offs, rt, ct, t1, ra):
    half = rt.shape[2] // 2
    rows = ra.shape[1] - 2 * SLOT
    lane = lax.broadcasted_iota(jnp.int32, (1, LANE), 1)
    for e in range(frames):
        rtaps = rt[e]
        ahead = lagged(ct[e], 256, -1, offs[e] + half - PAD)
        own = lagged(rtaps, LANE, 1, half)
        up = lagged(rtaps, LANE, 1, SLOT + half)
        down = lagged(rtaps, LANE, 1, half - rows)
        pair = []
        for k in range(count):
            one = slice(k, k + 1)
            band = toeplitz(ahead[one], LANE)
            at = slice(e * LANE, (e + 1) * LANE)
            t1[k, :LANE, at] = band[:, :LANE].astype(BF16)
            t1[k, LANE:, at] = band[:, LANE:].astype(BF16)
            side = (k % 2) * 64
            pair.append(
                jnp.concatenate(
                    [
                        toeplitz(own[one], rows, side),
                        toeplitz(up[one], SLOT, side),
                        toeplitz(down[one], SLOT, side),
                    ],
                    axis=0,
                )
            )
            if k % 2:
                both = jnp.where(lane < 64, pair[0], pair[1])
                ra[e, :, (k // 2) * LANE : (k // 2 + 1) * LANE] = both.astype(BF16)
                pair = []


def backward_tables(frames, count, rows, offs, rt, ct, t2, rb):
    half = rt.shape[2] // 2
    lane = lax.broadcasted_iota(jnp.int32, (1, LANE), 1)
    for e in range(frames):
        rtaps = rt[e]
        back = lagged(ct[e], 256, 1, offs[e] + half - PAD)
        own = lagged(rtaps, LANE, -1, half)
        above = lagged(rtaps, LANE, -1, SLOT + half)
        below = lagged(rtaps, LANE, -1, half - rows)
        for k in range(count):
            one = slice(k, k + 1)
            t2[k, e * LANE : (e + 1) * LANE, :] = toeplitz(back[one], LANE).astype(BF16)
            a = toeplitz(own[one], rows)
            b = toeplitz(above[one], rows, rows)
            c = toeplitz(below[one], rows, rows + SLOT)
            table = jnp.where(
                lane < rows,
                a,
                jnp.where(lane < rows + SLOT, b, jnp.where(lane < rows + 2 * SLOT, c, 0.0)),
            )
            rb[e, k * rows : (k + 1) * rows, :] = table.astype(BF16)


def mask_tables(cols, offs, valid, rowm, colm, mup_out, mdown_out):
    frames, rows = rowm.shape[:2]
    nblock = valid.shape[1]
    ups, downs = [], []
    for e in range(frames):
        row = lax.broadcasted_iota(jnp.int32, (rows, LANE), 0)
        block = row // (rows // nblock)
        mask = jnp.zeros((rows, LANE), F32)
        for b in range(nblock):
            mask = jnp.where(block == b, valid[e, b].astype(F32), mask)
        rowm[e] = mask
        ups.append(jnp.where(row < REACH, mask, 0.0)[:SLOT])
        downs.append(jnp.where(row >= rows - REACH, mask, 0.0)[rows - SLOT :])
        col = lax.broadcasted_iota(jnp.int32, (8, cols + LANE), 1) - PAD
        low = jnp.maximum(offs[e], 0)
        high = cols + jnp.minimum(offs[e], 0)
        colm[e] = jnp.where((col >= low) & (col < high), 1.0, 0.0)
    mup_out[...] = jnp.concatenate(ups, axis=0).astype(BF16)
    mdown_out[...] = jnp.concatenate(downs, axis=0).astype(BF16)


def main_kernel(
    n_sky, n_exp, offs, valid, rt, ct, sky_hbm, w_hbm, ex_hbm, out,
    sky, w, ex, t1, t2, ra, rb, rowm, colm, prod, blur, img, res, lift, own, grads, landed,
    up_out, down_out, up_in, down_in, mup_out, mdown_out, mup_in, mdown_in,
    s_send, s_recv, m_send, m_recv, g_send, g_recv, loads,
):
    count, rows, cols = w.shape
    frames = ex.shape[0]
    tall = rows + 2 * SLOT
    chunks = cols // CHUNK
    piece = cols // n_exp
    per = CHUNK // piece
    z = lax.axis_index("sky")
    me = lax.axis_index("exp")
    has_up = z > 0
    has_down = z < n_sky - 1
    first = me // per + 1

    def order(p):
        return lax.rem(first + p, chunks)

    def chunk(i):
        return pl.ds(pl.multiple_of(i * CHUNK, CHUNK), CHUNK)

    def load_w(i):
        at = chunk(i)
        return pltpu.make_async_copy(w_hbm.at[:, :, at], w.at[:, :, at], loads.at[i])

    load_sky = pltpu.make_async_copy(sky_hbm, sky, loads.at[chunks])
    load_ex = pltpu.make_async_copy(ex_hbm, ex, loads.at[chunks + 1])
    load_sky.start()
    load_w(order(chunks - 1)).start()
    load_w(order(0)).start()
    load_w(order(1)).start()
    load_ex.start()
    for p in range(2, chunks - 1):
        load_w(order(p)).start()

    barrier = pltpu.get_barrier_semaphore()

    @pl.when(has_up)
    def _():
        pl.semaphore_signal(barrier, inc=1, device_id={"sky": z - 1})

    @pl.when(has_down)
    def _():
        pl.semaphore_signal(barrier, inc=1, device_id={"sky": z + 1})

    for step in range(1, n_exp):
        pl.semaphore_signal(barrier, inc=1, device_id={"exp": lax.rem(me + step, n_exp)})

    prod[:, :, :LANE] = jnp.zeros((count, rows, LANE), BF16)
    prod[:, :, cols + LANE :] = jnp.zeros((count, rows, LANE), BF16)

    def multiply(i):
        load_w(i).wait()
        at = chunk(i)
        to = pl.ds(pl.multiple_of(i * CHUNK + LANE, LANE), CHUNK)
        model = sky[:, at]
        for k in range(count):
            prod[k, :, to] = w[k, :, at] * model

    def near(begin):
        return pl.ds(pl.multiple_of(begin, LANE), LANE)

    def lanes_of(i, blocks):
        start = i * CHUNK + (LANE if blocks == 4 else 0)
        return start, pl.ds(pl.multiple_of(start, LANE), blocks * LANE)

    def edge_copies(i, blocks):
        size = pl.ds(0, blocks * LANE)
        up = pltpu.make_async_remote_copy(
            src_ref=up_out.at[i, :, size], dst_ref=up_in.at[i, :, size],
            send_sem=s_send.at[0, i], recv_sem=s_recv.at[0, i], device_id={"sky": z - 1},
        )
        down = pltpu.make_async_remote_copy(
            src_ref=down_out.at[i, :, size], dst_ref=down_in.at[i, :, size],
            send_sem=s_send.at[1, i], recv_sem=s_recv.at[1, i], device_id={"sky": z + 1},
        )
        return up, down

    def mask_copies():
        up = pltpu.make_async_remote_copy(
            src_ref=mup_out, dst_ref=mup_in,
            send_sem=m_send.at[0], recv_sem=m_recv.at[0], device_id={"sky": z - 1},
        )
        down = pltpu.make_async_remote_copy(
            src_ref=mdown_out, dst_ref=mdown_in,
            send_sem=m_send.at[1], recv_sem=m_recv.at[1], device_id={"sky": z + 1},
        )
        return up, down

    def start(pair):
        @pl.when(has_up)
        def _():
            pair[0].start()

        @pl.when(has_down)
        def _():
            pair[1].start()

    def arrive(pair):
        @pl.when(has_down)
        def _():
            pair[0].wait_recv()

        @pl.when(has_up)
        def _():
            pair[1].wait_recv()

    def drain(pair):
        @pl.when(has_up)
        def _():
            pair[0].wait_send()

        @pl.when(has_down)
        def _():
            pair[1].wait_send()

    def row_of(width):
        return lax.broadcasted_iota(jnp.int32, (SLOT, width), 0)

    def forward(i, blocks):
        begin, lanes = lanes_of(i, blocks)
        width = blocks * LANE
        for k in range(count):
            left = jnp.concatenate(
                [
                    prod[k, :, pl.ds(pl.multiple_of(begin + j * LANE, LANE), 256)]
                    for j in range(blocks)
                ],
                axis=0,
            )
            got = jnp.dot(left, t1[k], preferred_element_type=F32).astype(BF16)
            for e in range(frames):
                for j in range(blocks):
                    blur[e, k * rows : (k + 1) * rows, j * LANE : (j + 1) * LANE] = got[
                        j * rows : (j + 1) * rows, e * LANE : (e + 1) * LANE
                    ]
        row = row_of(width)
        ups, downs = [], []
        for e in range(frames):
            image = jnp.dot(ra[e], blur[e, :, :width], preferred_element_type=F32)
            parts = [
                ex[e, :, chunk(i)],
                ex[e, :, near(jnp.minimum((i + 1) * CHUNK, cols - LANE))],
            ]
            if blocks == 5:
                parts = [ex[e, :, near(jnp.maximum(i * CHUNK - LANE, 0))]] + parts
            seen = jnp.concatenate(parts, axis=1)[:, PAD : PAD + width]
            value = image[:rows] - seen.astype(F32)
            img[e, :, lanes] = value
            up = image[rows : rows + SLOT]
            down = image[rows + SLOT :]
            head = jnp.where(row < REACH, value[:SLOT], 0.0)
            tail = jnp.where(row >= SLOT - REACH, value[rows - SLOT :], 0.0)
            ups += [head[:16], head[16:] + up[:8], up[8:]]
            downs += [down[:16], down[16:] + tail[:8], tail[8:]]
        up_out[i, :, :width] = jnp.concatenate(ups, axis=0).astype(BF16)
        down_out[i, :, :width] = jnp.concatenate(downs, axis=0).astype(BF16)

    def remain(i, blocks):
        begin, lanes = lanes_of(i, blocks)
        width = blocks * LANE
        arrive(edge_copies(i, blocks))
        above = down_in[i, :, :width].astype(F32)
        below = up_in[i, :, :width].astype(F32)
        mine_up = up_out[i, :, :width].astype(F32)
        mine_down = down_out[i, :, :width].astype(F32)
        mask_up = mdown_in[...].astype(F32)
        mask_down = mup_in[...].astype(F32)
        row = row_of(width)
        for e in range(frames):
            base = e * 2 * REACH
            image = img[e, :, lanes]
            slot = slice(e * SLOT, (e + 1) * SLOT)
            low = slice(base, base + SLOT)
            high = slice(base + 16, base + 16 + SLOT)
            value = jnp.concatenate(
                [
                    image[:SLOT] + jnp.where(row < REACH, above[low], 0.0),
                    image[SLOT : rows - SLOT],
                    image[rows - SLOT :] + jnp.where(row >= SLOT - REACH, below[high], 0.0),
                    above[high] + mine_up[high],
                    below[low] + mine_down[low],
                ],
                axis=0,
            )
            mask = jnp.concatenate([rowm[e], mask_up[slot], mask_down[slot]], axis=0)
            value = value * colm[e, :1, lanes] * jnp.tile(mask, (1, blocks))
            res[e, :tall, :width] = value.astype(BF16)
        for e in range(frames):
            got = jnp.dot(rb[e], res[e, :, :width], preferred_element_type=F32).astype(BF16)
            for k in range(count):
                for j in range(blocks):
                    to = pl.ds(pl.multiple_of((begin + j * LANE) * frames + e * LANE, LANE), LANE)
                    lift[k, :, to] = got[k * rows : (k + 1) * rows, j * LANE : (j + 1) * LANE]

    def backward(i):
        at = chunk(i)
        total = None
        for k in range(count):
            left = jnp.concatenate(
                [
                    lift[k, :, pl.ds(pl.multiple_of((i * CHUNK + j * LANE) * frames, LANE), frames * LANE)]
                    for j in range(CHUNK // LANE + 1)
                ],
                axis=0,
            )
            got = jnp.dot(left, t2[k], preferred_element_type=F32)
            lifted = jnp.concatenate(
                [
                    got[j * rows : (j + 1) * rows, LANE:] + got[(j + 1) * rows : (j + 2) * rows, :LANE]
                    for j in range(CHUNK // LANE)
                ],
                axis=1,
            )
            term = w[k, :, at].astype(F32) * lifted
            total = term if total is None else total + term
        for part in range(per):
            to = i * per + part
            value = total[:, part * piece : (part + 1) * piece]

            @pl.when(to == me)
            def _(value=value):
                own[...] = value

            @pl.when(to != me)
            def _(value=value, to=to):
                grads[to] = value.astype(BF16)
                gradient_copy(to).start()

    def gradient_copy(to):
        return pltpu.make_async_remote_copy(
            src_ref=grads.at[to], dst_ref=landed.at[me],
            send_sem=g_send.at[to], recv_sem=g_recv.at[me], device_id={"exp": to},
        )

    def both(p, stage):
        i = order(p)
        if isinstance(p, int) and p == 0:
            stage(i, 5)
            return

        @pl.when(i == 0)
        def _():
            stage(i, 5)

        @pl.when(i != 0)
        def _():
            stage(i, 4)

    def send(i, blocks):
        start(edge_copies(i, blocks))

    def ahead(i, blocks):
        forward(i, blocks)
        send(i, blocks)

    forward_tables(frames, count, offs, rt, ct, t1, ra)
    load_sky.wait()
    multiply(order(chunks - 1))
    multiply(order(0))
    multiply(order(1))
    load_ex.wait()
    forward(order(0), 5)
    neighbours = (z + n_sky - 1) // n_sky + (2 * n_sky - 2 - z) // n_sky
    pl.semaphore_wait(barrier, n_exp - 1 + neighbours)
    send(order(0), 5)

    @pl.loop(1, chunks)
    def _(p):
        @pl.when(p < chunks - 2)
        def _():
            multiply(order(p + 1))

        both(p, ahead)

    mask_tables(cols, offs, valid, rowm, colm, mup_out, mdown_out)
    start(mask_copies())

    @pl.when(jnp.logical_not(has_up))
    def _():
        down_in[...] = jnp.zeros(down_in.shape, BF16)
        mdown_in[...] = jnp.zeros(mdown_in.shape, BF16)

    @pl.when(jnp.logical_not(has_down))
    def _():
        up_in[...] = jnp.zeros(up_in.shape, BF16)
        mup_in[...] = jnp.zeros(mup_in.shape, BF16)

    for e in range(frames):
        res[e, tall:, :] = jnp.zeros((LANE - tall, CHUNK + LANE), BF16)
    backward_tables(frames, count, rows, offs, rt, ct, t2, rb)
    arrive(mask_copies())
    remain(order(0), 5)
    backward(order(0))

    @pl.loop(1, chunks)
    def _(p):
        both(p, remain)
        backward(order(p))

    out[...] = own[...]
    for step in range(1, n_exp):
        src = lax.rem(me + n_exp - step, n_exp)
        pltpu.make_async_remote_copy(
            src_ref=grads.at[src], dst_ref=landed.at[src],
            send_sem=g_send.at[src], recv_sem=g_recv.at[src], device_id={"exp": src},
        ).wait_recv()
        out[...] += landed[src].astype(F32)
    for step in range(1, n_exp):
        gradient_copy(lax.rem(me + step, n_exp)).wait_send()
    drain(mask_copies())

    def finish(i, blocks):
        drain(edge_copies(i, blocks))

    for p in range(chunks):
        both(p, finish)


def on_device(n_sky, n_exp, sky_model, eigen_weights, exposures, row_taps, col_taps, offsets, valid_blocks):
    count, rows, cols = eigen_weights.shape
    frames = exposures.shape[0]
    tall = rows + 2 * SLOT
    chunks = cols // CHUNK
    piece = cols // n_exp
    vmem = pl.BlockSpec(memory_space=pltpu.VMEM)
    smem = pl.BlockSpec(memory_space=pltpu.SMEM)
    edge = (chunks, frames * 2 * REACH, CHUNK + LANE)
    return pl.pallas_call(
        functools.partial(main_kernel, n_sky, n_exp),
        in_specs=[smem, smem, vmem, vmem] + [pl.BlockSpec(memory_space=pl.ANY)] * 3,
        out_specs=vmem,
        out_shape=pltpu.VMEM((rows, piece), F32),
        scratch_shapes=[
            pltpu.VMEM((rows, cols), BF16),
            pltpu.VMEM((count, rows, cols), BF16),
            pltpu.VMEM((frames, rows, cols), BF16),
            pltpu.VMEM((count, 256, frames * LANE), BF16),
            pltpu.VMEM((count, frames * LANE, 256), BF16),
            pltpu.VMEM((frames, tall, count * rows), BF16),
            pltpu.VMEM((frames, count * rows, LANE), BF16),
            pltpu.VMEM((frames, rows, LANE), F32),
            pltpu.VMEM((frames, 8, cols + LANE), F32),
            pltpu.VMEM((count, rows, cols + 2 * LANE), BF16),
            pltpu.VMEM((frames, count * rows, CHUNK + LANE), BF16),
            pltpu.VMEM((frames, rows, cols + LANE), F32),
            pltpu.VMEM((frames, LANE, CHUNK + LANE), BF16),
            pltpu.VMEM((count, rows, (cols + LANE) * frames), BF16),
            pltpu.VMEM((rows, piece), F32),
            pltpu.VMEM((n_exp, rows, piece), BF16),
            pltpu.VMEM((n_exp, rows, piece), BF16),
        ]
        + [pltpu.VMEM(edge, BF16)] * 4
        + [pltpu.VMEM((frames * SLOT, LANE), BF16)] * 4
        + [pltpu.SemaphoreType.DMA((2, chunks))] * 2
        + [pltpu.SemaphoreType.DMA((2,))] * 2
        + [pltpu.SemaphoreType.DMA((n_exp,))] * 2
        + [pltpu.SemaphoreType.DMA((chunks + 2,))],
        compiler_params=pltpu.CompilerParams(
            collective_id=0, has_side_effects=True, vmem_limit_bytes=60 * 1024 * 1024
        ),
        name="gradient",
    )(offsets, valid_blocks, row_taps, col_taps, sky_model, eigen_weights, exposures)


def solution(mesh):
    return jax.shard_map(
        functools.partial(on_device, mesh.shape["sky"], mesh.shape["exp"]),
        mesh=mesh,
        in_specs=(
            P("sky", None),
            P(None, "sky", None),
            P("exp", "sky", None),
            P("exp", None, None),
            P("exp", None, None),
            P("exp"),
            P("exp", "sky"),
        ),
        out_specs=P("sky", "exp"),
        check_vma=False,
    )
```

```python
import functools

import jax
import jax.numpy as jnp
from jax import lax
from jax.experimental import pallas as pl
from jax.experimental.pallas import tpu as pltpu
from jax.sharding import PartitionSpec as P

F32 = jnp.float32
BF16 = jnp.bfloat16
LANE = 128
PAD = 64
SLOT = 24
REACH = 20
BEHIND = 3
DEPTH = 2
CHUNK = 512


def lagged(taps, lanes, sign, start):
    width = taps.shape[1]
    lane = lax.broadcasted_iota(jnp.int32, (width, lanes), 1)
    lag = jnp.where(lane < lanes // 2, lane, lane - lanes)
    tap = lax.broadcasted_iota(jnp.int32, (width, lanes), 0)
    onehot = jnp.where(tap == sign * lag + start, 1.0, 0.0).astype(BF16)
    return jnp.dot(taps, onehot, preferred_element_type=F32)


def toeplitz(row, height, shift=0):
    full = jnp.broadcast_to(row, (height, row.shape[1]))
    return pltpu.roll(full, shift, 1, stride=1, stride_axis=0)


def forward_tables(frames, count, offs, rt, ct, t1, ra):
    half = rt.shape[2] // 2
    rows = ra.shape[1] - 2 * SLOT
    lane = lax.broadcasted_iota(jnp.int32, (1, LANE), 1)
    for e in range(frames):
        rtaps = rt[e]
        ahead = lagged(ct[e], 256, -1, offs[e] + half - PAD)
        own = lagged(rtaps, LANE, 1, half)
        up = lagged(rtaps, LANE, 1, SLOT + half)
        down = lagged(rtaps, LANE, 1, half - rows)
        pair = []
        for k in range(count):
            one = slice(k, k + 1)
            band = toeplitz(ahead[one], LANE)
            at = slice(e * LANE, (e + 1) * LANE)
            t1[k, :LANE, at] = band[:, :LANE].astype(BF16)
            t1[k, LANE:, at] = band[:, LANE:].astype(BF16)
            side = (k % 2) * 64
            pair.append(
                jnp.concatenate(
                    [
                        toeplitz(own[one], rows, side),
                        toeplitz(up[one], SLOT, side),
                        toeplitz(down[one], SLOT, side),
                    ],
                    axis=0,
                )
            )
            if k % 2:
                both = jnp.where(lane < 64, pair[0], pair[1])
                ra[e, :, (k // 2) * LANE : (k // 2 + 1) * LANE] = both.astype(BF16)
                pair = []


def backward_tables(frames, count, rows, offs, rt, ct, t2, rb):
    half = rt.shape[2] // 2
    lane = lax.broadcasted_iota(jnp.int32, (1, LANE), 1)
    for e in range(frames):
        rtaps = rt[e]
        back = lagged(ct[e], 256, 1, offs[e] + half - PAD)
        own = lagged(rtaps, LANE, -1, half)
        above = lagged(rtaps, LANE, -1, SLOT + half)
        below = lagged(rtaps, LANE, -1, half - rows)
        for k in range(count):
            one = slice(k, k + 1)
            t2[k, e * LANE : (e + 1) * LANE, :] = toeplitz(back[one], LANE).astype(BF16)
            a = toeplitz(own[one], rows)
            b = toeplitz(above[one], rows, rows)
            c = toeplitz(below[one], rows, rows + SLOT)
            table = jnp.where(
                lane < rows,
                a,
                jnp.where(lane < rows + SLOT, b, jnp.where(lane < rows + 2 * SLOT, c, 0.0)),
            )
            rb[e, k * rows : (k + 1) * rows, :] = table.astype(BF16)


def mask_tables(cols, offs, valid, rowm, colm, mup_out, mdown_out):
    frames, rows = rowm.shape[:2]
    nblock = valid.shape[1]
    ups, downs = [], []
    for e in range(frames):
        row = lax.broadcasted_iota(jnp.int32, (rows, LANE), 0)
        block = row // (rows // nblock)
        mask = jnp.zeros((rows, LANE), F32)
        for b in range(nblock):
            mask = jnp.where(block == b, valid[e, b].astype(F32), mask)
        rowm[e] = mask
        ups.append(jnp.where(row < REACH, mask, 0.0)[:SLOT])
        downs.append(jnp.where(row >= rows - REACH, mask, 0.0)[rows - SLOT :])
        col = lax.broadcasted_iota(jnp.int32, (8, cols + LANE), 1) - PAD
        low = jnp.maximum(offs[e], 0)
        high = cols + jnp.minimum(offs[e], 0)
        colm[e] = jnp.where((col >= low) & (col < high), 1.0, 0.0)
    mup_out[...] = jnp.concatenate(ups, axis=0).astype(BF16)
    mdown_out[...] = jnp.concatenate(downs, axis=0).astype(BF16)


def main_kernel(
    n_sky, n_exp, offs, valid, rt, ct, sky_hbm, w_hbm, ex_hbm, out,
    sky, w, ex, t1, t2, ra, rb, rowm, colm, prod, blur, img, res, lift, own, grads, landed,
    up_out, down_out, up_in, down_in, mup_out, mdown_out, mup_in, mdown_in,
    s_send, s_recv, m_send, m_recv, g_send, g_recv, loads,
):
    count, rows, cols = w.shape
    frames = ex.shape[0]
    tall = rows + 2 * SLOT
    chunks = cols // CHUNK
    piece = cols // n_exp
    per = CHUNK // piece
    z = lax.axis_index("sky")
    me = lax.axis_index("exp")
    has_up = z > 0
    has_down = z < n_sky - 1
    first = me // per + 1

    def order(p):
        return lax.rem(first + p, chunks)

    def chunk(i):
        return pl.ds(pl.multiple_of(i * CHUNK, CHUNK), CHUNK)

    def load_w(i):
        at = chunk(i)
        return pltpu.make_async_copy(w_hbm.at[:, :, at], w.at[:, :, at], loads.at[i])

    load_sky = pltpu.make_async_copy(sky_hbm, sky, loads.at[chunks])
    load_ex = pltpu.make_async_copy(ex_hbm, ex, loads.at[chunks + 1])
    load_sky.start()
    load_w(order(chunks - 1)).start()
    load_w(order(0)).start()
    load_w(order(1)).start()
    load_ex.start()
    for p in range(2, chunks - 1):
        load_w(order(p)).start()

    barrier = pltpu.get_barrier_semaphore()

    @pl.when(has_up)
    def _():
        pl.semaphore_signal(barrier, inc=1, device_id={"sky": z - 1})

    @pl.when(has_down)
    def _():
        pl.semaphore_signal(barrier, inc=1, device_id={"sky": z + 1})

    for step in range(1, n_exp):
        pl.semaphore_signal(barrier, inc=1, device_id={"exp": lax.rem(me + step, n_exp)})

    prod[:, :, :LANE] = jnp.zeros((count, rows, LANE), BF16)
    prod[:, :, cols + LANE :] = jnp.zeros((count, rows, LANE), BF16)

    def multiply(i):
        load_w(i).wait()
        at = chunk(i)
        to = pl.ds(pl.multiple_of(i * CHUNK + LANE, LANE), CHUNK)
        model = sky[:, at]
        for k in range(count):
            prod[k, :, to] = w[k, :, at] * model

    def near(begin):
        return pl.ds(pl.multiple_of(begin, LANE), LANE)

    def lanes_of(i, blocks):
        start = i * CHUNK + (LANE if blocks == 4 else 0)
        return start, pl.ds(pl.multiple_of(start, LANE), blocks * LANE)

    def edge_copies(i, blocks):
        size = pl.ds(0, blocks * LANE)
        up = pltpu.make_async_remote_copy(
            src_ref=up_out.at[i, :, size], dst_ref=up_in.at[i, :, size],
            send_sem=s_send.at[0, i], recv_sem=s_recv.at[0, i], device_id={"sky": z - 1},
        )
        down = pltpu.make_async_remote_copy(
            src_ref=down_out.at[i, :, size], dst_ref=down_in.at[i, :, size],
            send_sem=s_send.at[1, i], recv_sem=s_recv.at[1, i], device_id={"sky": z + 1},
        )
        return up, down

    def mask_copies():
        up = pltpu.make_async_remote_copy(
            src_ref=mup_out, dst_ref=mup_in,
            send_sem=m_send.at[0], recv_sem=m_recv.at[0], device_id={"sky": z - 1},
        )
        down = pltpu.make_async_remote_copy(
            src_ref=mdown_out, dst_ref=mdown_in,
            send_sem=m_send.at[1], recv_sem=m_recv.at[1], device_id={"sky": z + 1},
        )
        return up, down

    def start(pair):
        @pl.when(has_up)
        def _():
            pair[0].start()

        @pl.when(has_down)
        def _():
            pair[1].start()

    def arrive(pair):
        @pl.when(has_down)
        def _():
            pair[0].wait_recv()

        @pl.when(has_up)
        def _():
            pair[1].wait_recv()

    def drain(pair):
        @pl.when(has_up)
        def _():
            pair[0].wait_send()

        @pl.when(has_down)
        def _():
            pair[1].wait_send()

    def row_of(width):
        return lax.broadcasted_iota(jnp.int32, (SLOT, width), 0)

    def forward(i, blocks):
        begin, lanes = lanes_of(i, blocks)
        width = blocks * LANE
        for k in range(count):
            left = jnp.concatenate(
                [
                    prod[k, :, pl.ds(pl.multiple_of(begin + j * LANE, LANE), 256)]
                    for j in range(blocks)
                ],
                axis=0,
            )
            got = jnp.dot(left, t1[k], preferred_element_type=F32).astype(BF16)
            for e in range(frames):
                for j in range(blocks):
                    blur[e, k * rows : (k + 1) * rows, j * LANE : (j + 1) * LANE] = got[
                        j * rows : (j + 1) * rows, e * LANE : (e + 1) * LANE
                    ]
        row = row_of(width)
        ups, downs = [], []
        for e in range(frames):
            image = jnp.dot(ra[e], blur[e, :, :width], preferred_element_type=F32)
            parts = [
                ex[e, :, chunk(i)],
                ex[e, :, near(jnp.minimum((i + 1) * CHUNK, cols - LANE))],
            ]
            if blocks == 5:
                parts = [ex[e, :, near(jnp.maximum(i * CHUNK - LANE, 0))]] + parts
            seen = jnp.concatenate(parts, axis=1)[:, PAD : PAD + width]
            value = image[:rows] - seen.astype(F32)
            img[e, :, lanes] = value
            up = image[rows : rows + SLOT]
            down = image[rows + SLOT :]
            head = jnp.where(row < REACH, value[:SLOT], 0.0)
            tail = jnp.where(row >= SLOT - REACH, value[rows - SLOT :], 0.0)
            ups += [head[:16], head[16:] + up[:8], up[8:]]
            downs += [down[:16], down[16:] + tail[:8], tail[8:]]
        up_out[i, :, :width] = jnp.concatenate(ups, axis=0).astype(BF16)
        down_out[i, :, :width] = jnp.concatenate(downs, axis=0).astype(BF16)

    def remain(i, blocks):
        begin, lanes = lanes_of(i, blocks)
        width = blocks * LANE
        arrive(edge_copies(i, blocks))
        above = down_in[i, :, :width].astype(F32)
        below = up_in[i, :, :width].astype(F32)
        mine_up = up_out[i, :, :width].astype(F32)
        mine_down = down_out[i, :, :width].astype(F32)
        mask_up = mdown_in[...].astype(F32)
        mask_down = mup_in[...].astype(F32)
        row = row_of(width)
        for e in range(frames):
            base = e * 2 * REACH
            image = img[e, :, lanes]
            slot = slice(e * SLOT, (e + 1) * SLOT)
            low = slice(base, base + SLOT)
            high = slice(base + 16, base + 16 + SLOT)
            value = jnp.concatenate(
                [
                    image[:SLOT] + jnp.where(row < REACH, above[low], 0.0),
                    image[SLOT : rows - SLOT],
                    image[rows - SLOT :] + jnp.where(row >= SLOT - REACH, below[high], 0.0),
                    above[high] + mine_up[high],
                    below[low] + mine_down[low],
                ],
                axis=0,
            )
            mask = jnp.concatenate([rowm[e], mask_up[slot], mask_down[slot]], axis=0)
            value = value * colm[e, :1, lanes] * jnp.tile(mask, (1, blocks))
            res[e, :tall, :width] = value.astype(BF16)
        for e in range(frames):
            got = jnp.dot(rb[e], res[e, :, :width], preferred_element_type=F32).astype(BF16)
            for k in range(count):
                for j in range(blocks):
                    to = pl.ds(pl.multiple_of((begin + j * LANE) * frames + e * LANE, LANE), LANE)
                    lift[k, :, to] = got[k * rows : (k + 1) * rows, j * LANE : (j + 1) * LANE]

    def backward(i):
        at = chunk(i)
        total = None
        for k in range(count):
            left = jnp.concatenate(
                [
                    lift[k, :, pl.ds(pl.multiple_of((i * CHUNK + j * LANE) * frames, LANE), frames * LANE)]
                    for j in range(CHUNK // LANE + 1)
                ],
                axis=0,
            )
            got = jnp.dot(left, t2[k], preferred_element_type=F32)
            lifted = jnp.concatenate(
                [
                    got[j * rows : (j + 1) * rows, LANE:] + got[(j + 1) * rows : (j + 2) * rows, :LANE]
                    for j in range(CHUNK // LANE)
                ],
                axis=1,
            )
            term = w[k, :, at].astype(F32) * lifted
            total = term if total is None else total + term
        for part in range(per):
            to = i * per + part
            value = total[:, part * piece : (part + 1) * piece]

            @pl.when(to == me)
            def _(value=value):
                own[...] = value

            @pl.when(to != me)
            def _(value=value, to=to):
                grads[to] = value.astype(BF16)
                gradient_copy(to).start()

    def gradient_copy(to):
        return pltpu.make_async_remote_copy(
            src_ref=grads.at[to], dst_ref=landed.at[me],
            send_sem=g_send.at[to], recv_sem=g_recv.at[me], device_id={"exp": to},
        )

    def both(p, stage):
        i = order(p)
        wide = (i == 0) | (p == 0)

        @pl.when(wide)
        def _():
            stage(i, 5)

        @pl.when(jnp.logical_not(wide))
        def _():
            stage(i, 4)

    def send(i, blocks):
        start(edge_copies(i, blocks))

    def finish(i, blocks):
        drain(edge_copies(i, blocks))

    forward_tables(frames, count, offs, rt, ct, t1, ra)
    load_sky.wait()
    multiply(order(chunks - 1))
    multiply(order(0))
    load_ex.wait()

    @pl.loop(0, chunks + BEHIND)
    def _(p):
        @pl.when(p < chunks - 2)
        def _():
            multiply(order(p + 1))

        @pl.when(p < chunks)
        def _():
            both(p, forward)

        @pl.when(p == 0)
        def _():
            neighbours = (z + n_sky - 1) // n_sky + (2 * n_sky - 2 - z) // n_sky
            pl.semaphore_wait(barrier, n_exp - 1 + neighbours)

        @pl.when((p >= DEPTH) & (p < chunks))
        def _():
            both(p - DEPTH, finish)

        @pl.when(p < chunks)
        def _():
            both(p, send)

        @pl.when(p == 0)
        def _():
            mask_tables(cols, offs, valid, rowm, colm, mup_out, mdown_out)
            start(mask_copies())

            @pl.when(jnp.logical_not(has_up))
            def _():
                down_in[...] = jnp.zeros(down_in.shape, BF16)
                mdown_in[...] = jnp.zeros(mdown_in.shape, BF16)

            @pl.when(jnp.logical_not(has_down))
            def _():
                up_in[...] = jnp.zeros(up_in.shape, BF16)
                mup_in[...] = jnp.zeros(mup_in.shape, BF16)

            for e in range(frames):
                res[e, tall:, :] = jnp.zeros((LANE - tall, CHUNK + LANE), BF16)
            backward_tables(frames, count, rows, offs, rt, ct, t2, rb)
            arrive(mask_copies())

        @pl.when(p >= BEHIND)
        def _():
            both(p - BEHIND, remain)
            backward(order(p - BEHIND))

    out[...] = own[...]
    for step in range(1, n_exp):
        src = lax.rem(me + n_exp - step, n_exp)
        pltpu.make_async_remote_copy(
            src_ref=grads.at[src], dst_ref=landed.at[src],
            send_sem=g_send.at[src], recv_sem=g_recv.at[src], device_id={"exp": src},
        ).wait_recv()
        out[...] += landed[src].astype(F32)
    for step in range(1, n_exp):
        gradient_copy(lax.rem(me + step, n_exp)).wait_send()
    drain(mask_copies())

    for p in range(chunks - DEPTH, chunks):
        both(p, finish)


def on_device(n_sky, n_exp, sky_model, eigen_weights, exposures, row_taps, col_taps, offsets, valid_blocks):
    count, rows, cols = eigen_weights.shape
    frames = exposures.shape[0]
    tall = rows + 2 * SLOT
    chunks = cols // CHUNK
    piece = cols // n_exp
    vmem = pl.BlockSpec(memory_space=pltpu.VMEM)
    smem = pl.BlockSpec(memory_space=pltpu.SMEM)
    edge = (chunks, frames * 2 * REACH, CHUNK + LANE)
    return pl.pallas_call(
        functools.partial(main_kernel, n_sky, n_exp),
        in_specs=[smem, smem, vmem, vmem] + [pl.BlockSpec(memory_space=pl.ANY)] * 3,
        out_specs=vmem,
        out_shape=pltpu.VMEM((rows, piece), F32),
        scratch_shapes=[
            pltpu.VMEM((rows, cols), BF16),
            pltpu.VMEM((count, rows, cols), BF16),
            pltpu.VMEM((frames, rows, cols), BF16),
            pltpu.VMEM((count, 256, frames * LANE), BF16),
            pltpu.VMEM((count, frames * LANE, 256), BF16),
            pltpu.VMEM((frames, tall, count * rows), BF16),
            pltpu.VMEM((frames, count * rows, LANE), BF16),
            pltpu.VMEM((frames, rows, LANE), F32),
            pltpu.VMEM((frames, 8, cols + LANE), F32),
            pltpu.VMEM((count, rows, cols + 2 * LANE), BF16),
            pltpu.VMEM((frames, count * rows, CHUNK + LANE), BF16),
            pltpu.VMEM((frames, rows, cols + LANE), F32),
            pltpu.VMEM((frames, LANE, CHUNK + LANE), BF16),
            pltpu.VMEM((count, rows, (cols + LANE) * frames), BF16),
            pltpu.VMEM((rows, piece), F32),
            pltpu.VMEM((n_exp, rows, piece), BF16),
            pltpu.VMEM((n_exp, rows, piece), BF16),
        ]
        + [pltpu.VMEM(edge, BF16)] * 4
        + [pltpu.VMEM((frames * SLOT, LANE), BF16)] * 4
        + [pltpu.SemaphoreType.DMA((2, chunks))] * 2
        + [pltpu.SemaphoreType.DMA((2,))] * 2
        + [pltpu.SemaphoreType.DMA((n_exp,))] * 2
        + [pltpu.SemaphoreType.DMA((chunks + 2,))],
        compiler_params=pltpu.CompilerParams(
            collective_id=0, has_side_effects=True, vmem_limit_bytes=60 * 1024 * 1024
        ),
        name="gradient",
    )(offsets, valid_blocks, row_taps, col_taps, sky_model, eigen_weights, exposures)


def solution(mesh):
    return jax.shard_map(
        functools.partial(on_device, mesh.shape["sky"], mesh.shape["exp"]),
        mesh=mesh,
        in_specs=(
            P("sky", None),
            P(None, "sky", None),
            P("exp", "sky", None),
            P("exp", None, None),
            P("exp", None, None),
            P("exp"),
            P("exp", "sky"),
        ),
        out_specs=P("sky", "exp"),
        check_vma=False,
    )
```

```python
import functools

import jax
import jax.numpy as jnp
from jax import lax
from jax.experimental import pallas as pl
from jax.experimental.pallas import tpu as pltpu
from jax.sharding import PartitionSpec as P

F32 = jnp.float32
BF16 = jnp.bfloat16
LANE = 128
PAD = 64
SLOT = 24
REACH = 20
BEHIND = 3
DEPTH = 2
CHUNK = 512


def lagged(taps, lanes, sign, start):
    width = taps.shape[1]
    lane = lax.broadcasted_iota(jnp.int32, (width, lanes), 1)
    lag = jnp.where(lane < lanes // 2, lane, lane - lanes)
    tap = lax.broadcasted_iota(jnp.int32, (width, lanes), 0)
    onehot = jnp.where(tap == sign * lag + start, 1.0, 0.0).astype(BF16)
    return jnp.dot(taps, onehot, preferred_element_type=F32)


def toeplitz(row, height, shift=0):
    full = jnp.broadcast_to(row, (height, row.shape[1]))
    return pltpu.roll(full, shift, 1, stride=1, stride_axis=0)


def forward_tables(frames, count, offs, rt, ct, t1, ra):
    half = rt.shape[2] // 2
    rows = ra.shape[1] - 2 * SLOT
    lane = lax.broadcasted_iota(jnp.int32, (1, LANE), 1)
    for e in range(frames):
        rtaps = rt[e]
        ahead = lagged(ct[e], 256, -1, offs[e] + half - PAD)
        own = lagged(rtaps, LANE, 1, half)
        up = lagged(rtaps, LANE, 1, SLOT + half)
        down = lagged(rtaps, LANE, 1, half - rows)
        pair = []
        for k in range(count):
            one = slice(k, k + 1)
            band = toeplitz(ahead[one], LANE)
            at = slice(e * LANE, (e + 1) * LANE)
            t1[k, :LANE, at] = band[:, :LANE].astype(BF16)
            t1[k, LANE:, at] = band[:, LANE:].astype(BF16)
            side = (k % 2) * 64
            pair.append(
                jnp.concatenate(
                    [
                        toeplitz(own[one], rows, side),
                        toeplitz(up[one], SLOT, side),
                        toeplitz(down[one], SLOT, side),
                    ],
                    axis=0,
                )
            )
            if k % 2:
                both = jnp.where(lane < 64, pair[0], pair[1])
                ra[e, :, (k // 2) * LANE : (k // 2 + 1) * LANE] = both.astype(BF16)
                pair = []


def backward_tables(frames, count, rows, offs, rt, ct, t2, rb):
    half = rt.shape[2] // 2
    lane = lax.broadcasted_iota(jnp.int32, (1, LANE), 1)
    for e in range(frames):
        rtaps = rt[e]
        back = lagged(ct[e], 256, 1, offs[e] + half - PAD)
        own = lagged(rtaps, LANE, -1, half)
        above = lagged(rtaps, LANE, -1, SLOT + half)
        below = lagged(rtaps, LANE, -1, half - rows)
        for k in range(count):
            one = slice(k, k + 1)
            t2[k, e * LANE : (e + 1) * LANE, :] = toeplitz(back[one], LANE).astype(BF16)
            a = toeplitz(own[one], rows)
            b = toeplitz(above[one], rows, rows)
            c = toeplitz(below[one], rows, rows + SLOT)
            table = jnp.where(
                lane < rows,
                a,
                jnp.where(lane < rows + SLOT, b, jnp.where(lane < rows + 2 * SLOT, c, 0.0)),
            )
            rb[e, k * rows : (k + 1) * rows, :] = table.astype(BF16)


def mask_tables(cols, offs, valid, rowm, colm, mup_out, mdown_out):
    frames, rows = rowm.shape[:2]
    nblock = valid.shape[1]
    ups, downs = [], []
    for e in range(frames):
        row = lax.broadcasted_iota(jnp.int32, (rows, LANE), 0)
        block = row // (rows // nblock)
        mask = jnp.zeros((rows, LANE), F32)
        for b in range(nblock):
            mask = jnp.where(block == b, valid[e, b].astype(F32), mask)
        rowm[e] = mask
        ups.append(jnp.where(row < REACH, mask, 0.0)[:SLOT])
        downs.append(jnp.where(row >= rows - REACH, mask, 0.0)[rows - SLOT :])
        col = lax.broadcasted_iota(jnp.int32, (8, cols + LANE), 1) - PAD
        low = jnp.maximum(offs[e], 0)
        high = cols + jnp.minimum(offs[e], 0)
        colm[e] = jnp.where((col >= low) & (col < high), 1.0, 0.0)
    mup_out[...] = jnp.concatenate(ups, axis=0).astype(BF16)
    mdown_out[...] = jnp.concatenate(downs, axis=0).astype(BF16)


def main_kernel(
    n_sky, n_exp, offs_hbm, valid_hbm, rt_hbm, ct_hbm, sky_hbm, w_hbm, ex_hbm, out,
    offs, valid, rt, ct,
    sky, w, ex, t1, t2, ra, rb, rowm, colm, prod, blur, img, res, lift, own, grads, landed,
    up_out, down_out, up_in, down_in, mup_out, mdown_out, mup_in, mdown_in,
    s_send, s_recv, m_send, m_recv, g_send, g_recv, loads,
):
    count, rows, cols = w.shape
    frames = ex.shape[0]
    tall = rows + 2 * SLOT
    chunks = cols // CHUNK
    piece = cols // n_exp
    per = CHUNK // piece
    z = lax.axis_index("sky")
    me = lax.axis_index("exp")
    has_up = z > 0
    has_down = z < n_sky - 1
    first = me // per + 1

    def order(p):
        return lax.rem(first + p, chunks)

    def chunk(i):
        return pl.ds(pl.multiple_of(i * CHUNK, CHUNK), CHUNK)

    def load_w(i):
        at = chunk(i)
        return pltpu.make_async_copy(w_hbm.at[:, :, at], w.at[:, :, at], loads.at[i])

    load_sky = pltpu.make_async_copy(sky_hbm, sky, loads.at[chunks])
    load_ex = pltpu.make_async_copy(ex_hbm, ex, loads.at[chunks + 1])
    small = [
        pltpu.make_async_copy(src, dst, loads.at[chunks + 2 + n])
        for n, (src, dst) in enumerate(
            [(offs_hbm, offs), (rt_hbm, rt), (ct_hbm, ct), (valid_hbm, valid)]
        )
    ]
    for copy in small:
        copy.start()
    load_sky.start()
    load_w(order(chunks - 1)).start()
    load_w(order(0)).start()
    load_w(order(1)).start()
    load_ex.start()
    for p in range(2, chunks - 1):
        load_w(order(p)).start()

    barrier = pltpu.get_barrier_semaphore()

    @pl.when(has_up)
    def _():
        pl.semaphore_signal(barrier, inc=1, device_id={"sky": z - 1})

    @pl.when(has_down)
    def _():
        pl.semaphore_signal(barrier, inc=1, device_id={"sky": z + 1})

    for step in range(1, n_exp):
        pl.semaphore_signal(barrier, inc=1, device_id={"exp": lax.rem(me + step, n_exp)})

    prod[:, :, :LANE] = jnp.zeros((count, rows, LANE), BF16)
    prod[:, :, cols + LANE :] = jnp.zeros((count, rows, LANE), BF16)

    def multiply(i):
        load_w(i).wait()
        at = chunk(i)
        to = pl.ds(pl.multiple_of(i * CHUNK + LANE, LANE), CHUNK)
        model = sky[:, at]
        for k in range(count):
            prod[k, :, to] = w[k, :, at] * model

    def near(begin):
        return pl.ds(pl.multiple_of(begin, LANE), LANE)

    def lanes_of(i, blocks):
        start = i * CHUNK + (LANE if blocks == 4 else 0)
        return start, pl.ds(pl.multiple_of(start, LANE), blocks * LANE)

    def edge_copies(i, blocks):
        size = pl.ds(0, blocks * LANE)
        up = pltpu.make_async_remote_copy(
            src_ref=up_out.at[i, :, size], dst_ref=up_in.at[i, :, size],
            send_sem=s_send.at[0, i], recv_sem=s_recv.at[0, i], device_id={"sky": z - 1},
        )
        down = pltpu.make_async_remote_copy(
            src_ref=down_out.at[i, :, size], dst_ref=down_in.at[i, :, size],
            send_sem=s_send.at[1, i], recv_sem=s_recv.at[1, i], device_id={"sky": z + 1},
        )
        return up, down

    def mask_copies():
        up = pltpu.make_async_remote_copy(
            src_ref=mup_out, dst_ref=mup_in,
            send_sem=m_send.at[0], recv_sem=m_recv.at[0], device_id={"sky": z - 1},
        )
        down = pltpu.make_async_remote_copy(
            src_ref=mdown_out, dst_ref=mdown_in,
            send_sem=m_send.at[1], recv_sem=m_recv.at[1], device_id={"sky": z + 1},
        )
        return up, down

    def start(pair):
        @pl.when(has_up)
        def _():
            pair[0].start()

        @pl.when(has_down)
        def _():
            pair[1].start()

    def arrive(pair):
        @pl.when(has_down)
        def _():
            pair[0].wait_recv()

        @pl.when(has_up)
        def _():
            pair[1].wait_recv()

    def drain(pair):
        @pl.when(has_up)
        def _():
            pair[0].wait_send()

        @pl.when(has_down)
        def _():
            pair[1].wait_send()

    def row_of(width):
        return lax.broadcasted_iota(jnp.int32, (SLOT, width), 0)

    def forward(i, blocks):
        begin, lanes = lanes_of(i, blocks)
        width = blocks * LANE
        for k in range(count):
            left = jnp.concatenate(
                [
                    prod[k, :, pl.ds(pl.multiple_of(begin + j * LANE, LANE), 256)]
                    for j in range(blocks)
                ],
                axis=0,
            )
            got = jnp.dot(left, t1[k], preferred_element_type=F32).astype(BF16)
            for e in range(frames):
                for j in range(blocks):
                    blur[e, k * rows : (k + 1) * rows, j * LANE : (j + 1) * LANE] = got[
                        j * rows : (j + 1) * rows, e * LANE : (e + 1) * LANE
                    ]
        row = row_of(width)
        ups, downs = [], []
        for e in range(frames):
            image = jnp.dot(ra[e], blur[e, :, :width], preferred_element_type=F32)
            parts = [
                ex[e, :, chunk(i)],
                ex[e, :, near(jnp.minimum((i + 1) * CHUNK, cols - LANE))],
            ]
            if blocks == 5:
                parts = [ex[e, :, near(jnp.maximum(i * CHUNK - LANE, 0))]] + parts
            seen = jnp.concatenate(parts, axis=1)[:, PAD : PAD + width]
            value = image[:rows] - seen.astype(F32)
            img[e, :, lanes] = value
            up = image[rows : rows + SLOT]
            down = image[rows + SLOT :]
            head = jnp.where(row < REACH, value[:SLOT], 0.0)
            tail = jnp.where(row >= SLOT - REACH, value[rows - SLOT :], 0.0)
            ups += [head[:16], head[16:] + up[:8], up[8:]]
            downs += [down[:16], down[16:] + tail[:8], tail[8:]]
        up_out[i, :, :width] = jnp.concatenate(ups, axis=0).astype(BF16)
        down_out[i, :, :width] = jnp.concatenate(downs, axis=0).astype(BF16)

    def remain(i, blocks):
        begin, lanes = lanes_of(i, blocks)
        width = blocks * LANE
        arrive(edge_copies(i, blocks))
        above = down_in[i, :, :width].astype(F32)
        below = up_in[i, :, :width].astype(F32)
        mine_up = up_out[i, :, :width].astype(F32)
        mine_down = down_out[i, :, :width].astype(F32)
        mask_up = mdown_in[...].astype(F32)
        mask_down = mup_in[...].astype(F32)
        row = row_of(width)
        for e in range(frames):
            base = e * 2 * REACH
            image = img[e, :, lanes]
            slot = slice(e * SLOT, (e + 1) * SLOT)
            low = slice(base, base + SLOT)
            high = slice(base + 16, base + 16 + SLOT)
            value = jnp.concatenate(
                [
                    image[:SLOT] + jnp.where(row < REACH, above[low], 0.0),
                    image[SLOT : rows - SLOT],
                    image[rows - SLOT :] + jnp.where(row >= SLOT - REACH, below[high], 0.0),
                    above[high] + mine_up[high],
                    below[low] + mine_down[low],
                ],
                axis=0,
            )
            mask = jnp.concatenate([rowm[e], mask_up[slot], mask_down[slot]], axis=0)
            value = value * colm[e, :1, lanes] * jnp.tile(mask, (1, blocks))
            res[e, :tall, :width] = value.astype(BF16)
        for e in range(frames):
            got = jnp.dot(rb[e], res[e, :, :width], preferred_element_type=F32).astype(BF16)
            for k in range(count):
                for j in range(blocks):
                    to = pl.ds(pl.multiple_of((begin + j * LANE) * frames + e * LANE, LANE), LANE)
                    lift[k, :, to] = got[k * rows : (k + 1) * rows, j * LANE : (j + 1) * LANE]

    def backward(i):
        at = chunk(i)
        total = None
        for k in range(count):
            left = jnp.concatenate(
                [
                    lift[k, :, pl.ds(pl.multiple_of((i * CHUNK + j * LANE) * frames, LANE), frames * LANE)]
                    for j in range(CHUNK // LANE + 1)
                ],
                axis=0,
            )
            got = jnp.dot(left, t2[k], preferred_element_type=F32)
            lifted = jnp.concatenate(
                [
                    got[j * rows : (j + 1) * rows, LANE:] + got[(j + 1) * rows : (j + 2) * rows, :LANE]
                    for j in range(CHUNK // LANE)
                ],
                axis=1,
            )
            term = w[k, :, at].astype(F32) * lifted
            total = term if total is None else total + term
        for part in range(per):
            to = i * per + part
            value = total[:, part * piece : (part + 1) * piece]

            @pl.when(to == me)
            def _(value=value):
                own[...] = value

            @pl.when(to != me)
            def _(value=value, to=to):
                grads[to] = value.astype(BF16)
                gradient_copy(to).start()

    def gradient_copy(to):
        return pltpu.make_async_remote_copy(
            src_ref=grads.at[to], dst_ref=landed.at[me],
            send_sem=g_send.at[to], recv_sem=g_recv.at[me], device_id={"exp": to},
        )

    def both(p, stage):
        i = order(p)
        wide = (i == 0) | (p == 0)

        @pl.when(wide)
        def _():
            stage(i, 5)

        @pl.when(jnp.logical_not(wide))
        def _():
            stage(i, 4)

    def send(i, blocks):
        start(edge_copies(i, blocks))

    def finish(i, blocks):
        drain(edge_copies(i, blocks))

    for copy in small:
        copy.wait()
    forward_tables(frames, count, offs, rt, ct, t1, ra)
    load_sky.wait()
    multiply(order(chunks - 1))
    multiply(order(0))
    load_ex.wait()

    @pl.loop(0, chunks + BEHIND)
    def _(p):
        @pl.when(p < chunks - 2)
        def _():
            multiply(order(p + 1))

        @pl.when(p < chunks)
        def _():
            both(p, forward)

        @pl.when(p == 0)
        def _():
            neighbours = (z + n_sky - 1) // n_sky + (2 * n_sky - 2 - z) // n_sky
            pl.semaphore_wait(barrier, n_exp - 1 + neighbours)

        @pl.when((p >= DEPTH) & (p < chunks))
        def _():
            both(p - DEPTH, finish)

        @pl.when(p < chunks)
        def _():
            both(p, send)

        @pl.when(p == 0)
        def _():
            mask_tables(cols, offs, valid, rowm, colm, mup_out, mdown_out)
            start(mask_copies())

            @pl.when(jnp.logical_not(has_up))
            def _():
                down_in[...] = jnp.zeros(down_in.shape, BF16)
                mdown_in[...] = jnp.zeros(mdown_in.shape, BF16)

            @pl.when(jnp.logical_not(has_down))
            def _():
                up_in[...] = jnp.zeros(up_in.shape, BF16)
                mup_in[...] = jnp.zeros(mup_in.shape, BF16)

            for e in range(frames):
                res[e, tall:, :] = jnp.zeros((LANE - tall, CHUNK + LANE), BF16)
            backward_tables(frames, count, rows, offs, rt, ct, t2, rb)

        @pl.when(p == BEHIND)
        def _():
            arrive(mask_copies())

        @pl.when(p >= BEHIND)
        def _():
            both(p - BEHIND, remain)
            backward(order(p - BEHIND))

    out[...] = own[...]
    for step in range(1, n_exp):
        src = lax.rem(me + n_exp - step, n_exp)
        pltpu.make_async_remote_copy(
            src_ref=grads.at[src], dst_ref=landed.at[src],
            send_sem=g_send.at[src], recv_sem=g_recv.at[src], device_id={"exp": src},
        ).wait_recv()
        out[...] += landed[src].astype(F32)
    for step in range(1, n_exp):
        gradient_copy(lax.rem(me + step, n_exp)).wait_send()
    drain(mask_copies())

    for p in range(chunks - DEPTH, chunks):
        both(p, finish)


def on_device(n_sky, n_exp, sky_model, eigen_weights, exposures, row_taps, col_taps, offsets, valid_blocks):
    count, rows, cols = eigen_weights.shape
    frames = exposures.shape[0]
    tall = rows + 2 * SLOT
    chunks = cols // CHUNK
    piece = cols // n_exp
    vmem = pl.BlockSpec(memory_space=pltpu.VMEM)
    edge = (chunks, frames * 2 * REACH, CHUNK + LANE)
    return pl.pallas_call(
        functools.partial(main_kernel, n_sky, n_exp),
        in_specs=[pl.BlockSpec(memory_space=pl.ANY)] * 7,
        out_specs=vmem,
        out_shape=pltpu.VMEM((rows, piece), F32),
        scratch_shapes=[
            pltpu.SMEM(offsets.shape, jnp.int32),
            pltpu.SMEM(valid_blocks.shape, jnp.int32),
            pltpu.VMEM(row_taps.shape, BF16),
            pltpu.VMEM(col_taps.shape, BF16),
            pltpu.VMEM((rows, cols), BF16),
            pltpu.VMEM((count, rows, cols), BF16),
            pltpu.VMEM((frames, rows, cols), BF16),
            pltpu.VMEM((count, 256, frames * LANE), BF16),
            pltpu.VMEM((count, frames * LANE, 256), BF16),
            pltpu.VMEM((frames, tall, count * rows), BF16),
            pltpu.VMEM((frames, count * rows, LANE), BF16),
            pltpu.VMEM((frames, rows, LANE), F32),
            pltpu.VMEM((frames, 8, cols + LANE), F32),
            pltpu.VMEM((count, rows, cols + 2 * LANE), BF16),
            pltpu.VMEM((frames, count * rows, CHUNK + LANE), BF16),
            pltpu.VMEM((frames, rows, cols + LANE), F32),
            pltpu.VMEM((frames, LANE, CHUNK + LANE), BF16),
            pltpu.VMEM((count, rows, (cols + LANE) * frames), BF16),
            pltpu.VMEM((rows, piece), F32),
            pltpu.VMEM((n_exp, rows, piece), BF16),
            pltpu.VMEM((n_exp, rows, piece), BF16),
        ]
        + [pltpu.VMEM(edge, BF16)] * 4
        + [pltpu.VMEM((frames * SLOT, LANE), BF16)] * 4
        + [pltpu.SemaphoreType.DMA((2, chunks))] * 2
        + [pltpu.SemaphoreType.DMA((2,))] * 2
        + [pltpu.SemaphoreType.DMA((n_exp,))] * 2
        + [pltpu.SemaphoreType.DMA((chunks + 6,))],
        compiler_params=pltpu.CompilerParams(
            collective_id=0, has_side_effects=True, vmem_limit_bytes=60 * 1024 * 1024
        ),
        name="gradient",
    )(offsets, valid_blocks, row_taps, col_taps, sky_model, eigen_weights, exposures)


def solution(mesh):
    return jax.shard_map(
        functools.partial(on_device, mesh.shape["sky"], mesh.shape["exp"]),
        mesh=mesh,
        in_specs=(
            P("sky", None),
            P(None, "sky", None),
            P("exp", "sky", None),
            P("exp", None, None),
            P("exp", None, None),
            P("exp"),
            P("exp", "sky"),
        ),
        out_specs=P("sky", "exp"),
        check_vma=False,
    )
```

```python
import functools

import jax
import jax.numpy as jnp
from jax import lax
from jax.experimental import pallas as pl
from jax.experimental.pallas import tpu as pltpu
from jax.sharding import PartitionSpec as P

F32 = jnp.float32
BF16 = jnp.bfloat16
LANE = 128
PAD = 64
SLOT = 24
REACH = 20
BEHIND = 3
DEPTH = 2
CHUNK = 512


def lagged(taps, lanes, sign, start):
    width = taps.shape[1]
    lane = lax.broadcasted_iota(jnp.int32, (width, lanes), 1)
    lag = jnp.where(lane < lanes // 2, lane, lane - lanes)
    tap = lax.broadcasted_iota(jnp.int32, (width, lanes), 0)
    onehot = jnp.where(tap == sign * lag + start, 1.0, 0.0).astype(BF16)
    return jnp.dot(taps, onehot, preferred_element_type=F32)


def toeplitz(row, height, shift=0):
    full = jnp.broadcast_to(row, (height, row.shape[1]))
    return pltpu.roll(full, shift, 1, stride=1, stride_axis=0)


def forward_tables(frames, count, offs, rt, ct, t1, ra):
    half = rt.shape[2] // 2
    rows = ra.shape[1] - 2 * SLOT
    lane = lax.broadcasted_iota(jnp.int32, (1, LANE), 1)
    for e in range(frames):
        rtaps = rt[e]
        ahead = lagged(ct[e], 256, -1, offs[e] + half - PAD)
        own = lagged(rtaps, LANE, 1, half)
        up = lagged(rtaps, LANE, 1, SLOT + half)
        down = lagged(rtaps, LANE, 1, half - rows)
        pair = []
        for k in range(count):
            one = slice(k, k + 1)
            band = toeplitz(ahead[one], LANE)
            at = slice(e * LANE, (e + 1) * LANE)
            t1[k, :LANE, at] = band[:, :LANE].astype(BF16)
            t1[k, LANE:, at] = band[:, LANE:].astype(BF16)
            side = (k % 2) * 64
            pair.append(
                jnp.concatenate(
                    [
                        toeplitz(own[one], rows, side),
                        toeplitz(up[one], SLOT, side),
                        toeplitz(down[one], SLOT, side),
                    ],
                    axis=0,
                )
            )
            if k % 2:
                both = jnp.where(lane < 64, pair[0], pair[1])
                ra[e, :, (k // 2) * LANE : (k // 2 + 1) * LANE] = both.astype(BF16)
                pair = []


def backward_tables(frames, count, rows, offs, rt, ct, t2, rb):
    half = rt.shape[2] // 2
    lane = lax.broadcasted_iota(jnp.int32, (1, LANE), 1)
    for e in range(frames):
        rtaps = rt[e]
        back = lagged(ct[e], 256, 1, offs[e] + half - PAD)
        own = lagged(rtaps, LANE, -1, half)
        above = lagged(rtaps, LANE, -1, SLOT + half)
        below = lagged(rtaps, LANE, -1, half - rows)
        for k in range(count):
            one = slice(k, k + 1)
            t2[k, e * LANE : (e + 1) * LANE, :] = toeplitz(back[one], LANE).astype(BF16)
            a = toeplitz(own[one], rows)
            b = toeplitz(above[one], rows, rows)
            c = toeplitz(below[one], rows, rows + SLOT)
            table = jnp.where(
                lane < rows,
                a,
                jnp.where(lane < rows + SLOT, b, jnp.where(lane < rows + 2 * SLOT, c, 0.0)),
            )
            rb[e, k * rows : (k + 1) * rows, :] = table.astype(BF16)


def mask_tables(cols, offs, valid, rowm, colm, mup_out, mdown_out):
    frames, rows = rowm.shape[:2]
    nblock = valid.shape[1]
    ups, downs = [], []
    for e in range(frames):
        row = lax.broadcasted_iota(jnp.int32, (rows, LANE), 0)
        block = row // (rows // nblock)
        mask = jnp.zeros((rows, LANE), F32)
        for b in range(nblock):
            mask = jnp.where(block == b, valid[e, b].astype(F32), mask)
        rowm[e] = mask
        ups.append(jnp.where(row < REACH, mask, 0.0)[:SLOT])
        downs.append(jnp.where(row >= rows - REACH, mask, 0.0)[rows - SLOT :])
        col = lax.broadcasted_iota(jnp.int32, (8, cols + LANE), 1) - PAD
        low = jnp.maximum(offs[e], 0)
        high = cols + jnp.minimum(offs[e], 0)
        colm[e] = jnp.where((col >= low) & (col < high), 1.0, 0.0)
    mup_out[...] = jnp.concatenate(ups, axis=0).astype(BF16)
    mdown_out[...] = jnp.concatenate(downs, axis=0).astype(BF16)


def main_kernel(
    n_sky, n_exp, offs_hbm, valid_hbm, rt_hbm, ct_hbm, sky_hbm, w_hbm, ex_hbm, out,
    offs, valid, rt, ct,
    sky, w, ex, t1, t2, ra, rb, rowm, colm, prod, blur, img, res, lift, own, grads, landed,
    up_out, down_out, up_in, down_in, mup_out, mdown_out, mup_in, mdown_in,
    s_send, s_recv, m_send, m_recv, g_send, g_recv, loads,
):
    count, rows, cols = w.shape
    frames = ex.shape[0]
    tall = rows + 2 * SLOT
    chunks = cols // CHUNK
    piece = cols // n_exp
    per = CHUNK // piece
    z = lax.axis_index("sky")
    me = lax.axis_index("exp")
    has_up = z > 0
    has_down = z < n_sky - 1
    chip = me // 2
    rising = lax.rem(chip, 2)
    base = 2 * chip + rising if per == 1 else me // per
    far = (me != base) & (per == 1)

    def walk(p):
        return lax.rem(base + (2 * rising - 1) * (1 + p) + 2 * chunks, chunks)

    def order(p):
        return walk(jnp.where(far & (p >= chunks - 2), 2 * chunks - 3 - p, p))

    def chunk(i):
        return pl.ds(pl.multiple_of(i * CHUNK, CHUNK), CHUNK)

    def load_w(i):
        at = chunk(i)
        return pltpu.make_async_copy(w_hbm.at[:, :, at], w.at[:, :, at], loads.at[i])

    load_sky = pltpu.make_async_copy(sky_hbm, sky, loads.at[chunks])
    load_ex = pltpu.make_async_copy(ex_hbm, ex, loads.at[chunks + 1])
    barrier = pltpu.get_barrier_semaphore()

    @pl.when(has_up)
    def _():
        pl.semaphore_signal(barrier, inc=1, device_id={"sky": z - 1})

    @pl.when(has_down)
    def _():
        pl.semaphore_signal(barrier, inc=1, device_id={"sky": z + 1})

    for step in range(1, n_exp):
        pl.semaphore_signal(barrier, inc=1, device_id={"exp": lax.rem(me + step, n_exp)})

    small = [
        pltpu.make_async_copy(src, dst, loads.at[chunks + 2 + n])
        for n, (src, dst) in enumerate(
            [(offs_hbm, offs), (rt_hbm, rt), (ct_hbm, ct), (valid_hbm, valid)]
        )
    ]
    for copy in small:
        copy.start()
    load_sky.start()
    load_w(walk(chunks - 1)).start()
    load_w(walk(0)).start()
    load_w(walk(1)).start()
    load_ex.start()
    for p in range(2, chunks - 1):
        load_w(walk(p)).start()

    prod[:, :, :LANE] = jnp.zeros((count, rows, LANE), BF16)
    prod[:, :, cols + LANE :] = jnp.zeros((count, rows, LANE), BF16)

    def multiply(i):
        load_w(i).wait()
        at = chunk(i)
        to = pl.ds(pl.multiple_of(i * CHUNK + LANE, LANE), CHUNK)
        model = sky[:, at]
        for k in range(count):
            prod[k, :, to] = w[k, :, at] * model

    def near(begin):
        return pl.ds(pl.multiple_of(begin, LANE), LANE)

    def lanes_of(i, blocks):
        swapped = far & (i == order(chunks - 2))
        side = jnp.where(swapped, 1 - rising, rising)
        start = i * CHUNK + {3: LANE, 4: side * LANE, 5: 0}[blocks]
        return start, pl.ds(pl.multiple_of(start, LANE), blocks * LANE)

    def edge_copies(i, blocks):
        size = pl.ds(0, blocks * LANE)
        up = pltpu.make_async_remote_copy(
            src_ref=up_out.at[i, :, size], dst_ref=up_in.at[i, :, size],
            send_sem=s_send.at[0, i], recv_sem=s_recv.at[0, i], device_id={"sky": z - 1},
        )
        down = pltpu.make_async_remote_copy(
            src_ref=down_out.at[i, :, size], dst_ref=down_in.at[i, :, size],
            send_sem=s_send.at[1, i], recv_sem=s_recv.at[1, i], device_id={"sky": z + 1},
        )
        return up, down

    def mask_copies():
        up = pltpu.make_async_remote_copy(
            src_ref=mup_out, dst_ref=mup_in,
            send_sem=m_send.at[0], recv_sem=m_recv.at[0], device_id={"sky": z - 1},
        )
        down = pltpu.make_async_remote_copy(
            src_ref=mdown_out, dst_ref=mdown_in,
            send_sem=m_send.at[1], recv_sem=m_recv.at[1], device_id={"sky": z + 1},
        )
        return up, down

    def start(pair):
        @pl.when(has_up)
        def _():
            pair[0].start()

        @pl.when(has_down)
        def _():
            pair[1].start()

    def arrive(pair):
        @pl.when(has_down)
        def _():
            pair[0].wait_recv()

        @pl.when(has_up)
        def _():
            pair[1].wait_recv()

    def drain(pair):
        @pl.when(has_up)
        def _():
            pair[0].wait_send()

        @pl.when(has_down)
        def _():
            pair[1].wait_send()

    def row_of(width):
        return lax.broadcasted_iota(jnp.int32, (SLOT, width), 0)

    def forward(i, blocks):
        begin, lanes = lanes_of(i, blocks)
        width = blocks * LANE
        for k in range(count):
            left = jnp.concatenate(
                [
                    prod[k, :, pl.ds(pl.multiple_of(begin + j * LANE, LANE), 256)]
                    for j in range(blocks)
                ],
                axis=0,
            )
            got = jnp.dot(left, t1[k], preferred_element_type=F32).astype(BF16)
            for e in range(frames):
                for j in range(blocks):
                    blur[e, k * rows : (k + 1) * rows, j * LANE : (j + 1) * LANE] = got[
                        j * rows : (j + 1) * rows, e * LANE : (e + 1) * LANE
                    ]
        row = row_of(width)
        ups, downs = [], []
        for e in range(frames):
            image = jnp.dot(ra[e], blur[e, :, :width], preferred_element_type=F32)
            parts = [
                ex[e, :, near(jnp.clip(begin + (j - 1) * LANE, 0, cols - LANE))]
                for j in range(blocks + 1)
            ]
            seen = jnp.concatenate(parts, axis=1)[:, PAD : PAD + width]
            value = image[:rows] - seen.astype(F32)
            img[e, :, lanes] = value
            up = image[rows : rows + SLOT]
            down = image[rows + SLOT :]
            head = jnp.where(row < REACH, value[:SLOT], 0.0)
            tail = jnp.where(row >= SLOT - REACH, value[rows - SLOT :], 0.0)
            ups += [head[:16], head[16:] + up[:8], up[8:]]
            downs += [down[:16], down[16:] + tail[:8], tail[8:]]
        up_out[i, :, :width] = jnp.concatenate(ups, axis=0).astype(BF16)
        down_out[i, :, :width] = jnp.concatenate(downs, axis=0).astype(BF16)

    def remain(i, blocks):
        begin, lanes = lanes_of(i, blocks)
        width = blocks * LANE
        arrive(edge_copies(i, blocks))
        above = down_in[i, :, :width].astype(F32)
        below = up_in[i, :, :width].astype(F32)
        mine_up = up_out[i, :, :width].astype(F32)
        mine_down = down_out[i, :, :width].astype(F32)
        mask_up = mdown_in[...].astype(F32)
        mask_down = mup_in[...].astype(F32)
        row = row_of(width)
        for e in range(frames):
            base = e * 2 * REACH
            image = img[e, :, lanes]
            slot = slice(e * SLOT, (e + 1) * SLOT)
            low = slice(base, base + SLOT)
            high = slice(base + 16, base + 16 + SLOT)
            value = jnp.concatenate(
                [
                    image[:SLOT] + jnp.where(row < REACH, above[low], 0.0),
                    image[SLOT : rows - SLOT],
                    image[rows - SLOT :] + jnp.where(row >= SLOT - REACH, below[high], 0.0),
                    above[high] + mine_up[high],
                    below[low] + mine_down[low],
                ],
                axis=0,
            )
            mask = jnp.concatenate([rowm[e], mask_up[slot], mask_down[slot]], axis=0)
            value = value * colm[e, :1, lanes] * jnp.tile(mask, (1, blocks))
            res[e, :tall, :width] = value.astype(BF16)
            got = jnp.dot(rb[e], res[e, :, :width], preferred_element_type=F32).astype(BF16)
            for k in range(count):
                for j in range(blocks):
                    to = pl.ds(pl.multiple_of((begin + j * LANE) * frames + e * LANE, LANE), LANE)
                    lift[k, :, to] = got[k * rows : (k + 1) * rows, j * LANE : (j + 1) * LANE]

    def backward(i):
        at = chunk(i)
        total = None
        for k in range(count):
            left = jnp.concatenate(
                [
                    lift[k, :, pl.ds(pl.multiple_of((i * CHUNK + j * LANE) * frames, LANE), frames * LANE)]
                    for j in range(CHUNK // LANE + 1)
                ],
                axis=0,
            )
            got = jnp.dot(left, t2[k], preferred_element_type=F32)
            lifted = jnp.concatenate(
                [
                    got[j * rows : (j + 1) * rows, LANE:] + got[(j + 1) * rows : (j + 2) * rows, :LANE]
                    for j in range(CHUNK // LANE)
                ],
                axis=1,
            )
            term = w[k, :, at].astype(F32) * lifted
            total = term if total is None else total + term
        for part in range(per):
            to = i * per + part
            value = total[:, part * piece : (part + 1) * piece]

            @pl.when(to == me)
            def _(value=value):
                own[...] = value

            @pl.when(to != me)
            def _(value=value, to=to):
                grads[to] = value.astype(BF16)
                gradient_copy(to).start()

    def gradient_copy(to):
        return pltpu.make_async_remote_copy(
            src_ref=grads.at[to], dst_ref=landed.at[me],
            send_sem=g_send.at[to], recv_sem=g_recv.at[me], device_id={"exp": to},
        )

    def collect(begin, end):
        for q in range(begin, end):
            step = n_exp // 2 - 1 - q // 2
            there = lax.rem(chip + (1 - 2 * rising) * step + n_exp // 2, n_exp // 2)
            src = 2 * there + q % 2 if step else me + 1 - 2 * lax.rem(me, 2)
            pltpu.make_async_remote_copy(
                src_ref=grads.at[src], dst_ref=landed.at[src],
                send_sem=g_send.at[src], recv_sem=g_recv.at[src], device_id={"exp": src},
            ).wait_recv()
            piece_sum = landed[src].astype(F32)
            out[...] = piece_sum if q == 0 else out[...] + piece_sum

    early = n_exp - 4 if per == 1 else 0

    def both(p, stage):
        i = order(p)
        edge = (1 - rising) * (chunks - 1)
        wraps = order(0) == edge
        wide = (i == edge) | (p == 0) | (far & wraps & (p == chunks - 2))
        narrow = (p == chunks - 1) & (i != edge) & (far | jnp.logical_not(wraps))

        @pl.when(wide)
        def _():
            stage(i, 5)

        @pl.when(jnp.logical_not(wide | narrow))
        def _():
            stage(i, 4)

        @pl.when(narrow)
        def _():
            stage(i, 3)

    def send(i, blocks):
        start(edge_copies(i, blocks))

    def finish(i, blocks):
        drain(edge_copies(i, blocks))

    for copy in small:
        copy.wait()
    forward_tables(frames, count, offs, rt, ct, t1, ra)
    load_sky.wait()
    multiply(walk(chunks - 1))
    multiply(walk(0))
    load_ex.wait()

    @pl.loop(0, chunks + BEHIND)
    def _(p):
        @pl.when(p < chunks - 2)
        def _():
            multiply(walk(p + 1))

        @pl.when(p < chunks)
        def _():
            both(p, forward)

        @pl.when(p == 0)
        def _():
            neighbours = (z + n_sky - 1) // n_sky + (2 * n_sky - 2 - z) // n_sky
            pl.semaphore_wait(barrier, n_exp - 1 + neighbours)

        @pl.when((p >= DEPTH) & (p < chunks))
        def _():
            both(p - DEPTH, finish)

        @pl.when(p < chunks)
        def _():
            both(p, send)

        @pl.when(p == 0)
        def _():
            mask_tables(cols, offs, valid, rowm, colm, mup_out, mdown_out)
            start(mask_copies())

            @pl.when(jnp.logical_not(has_up))
            def _():
                down_in[...] = jnp.zeros(down_in.shape, BF16)
                mdown_in[...] = jnp.zeros(mdown_in.shape, BF16)

            @pl.when(jnp.logical_not(has_down))
            def _():
                up_in[...] = jnp.zeros(up_in.shape, BF16)
                mup_in[...] = jnp.zeros(mup_in.shape, BF16)

            for e in range(frames):
                res[e, tall:, :] = jnp.zeros((LANE - tall, CHUNK + LANE), BF16)
            backward_tables(frames, count, rows, offs, rt, ct, t2, rb)

        @pl.when(p == BEHIND)
        def _():
            arrive(mask_copies())

        @pl.when(p == chunks + BEHIND - 1)
        def _():
            collect(0, early)

        @pl.when(p >= BEHIND)
        def _():
            both(p - BEHIND, remain)
            backward(order(p - BEHIND))

    collect(early, n_exp - 1)
    out[...] = out[...] + own[...]
    for step in range(1, n_exp):
        gradient_copy(lax.rem(me + step, n_exp)).wait_send()
    drain(mask_copies())

    for p in range(chunks - DEPTH, chunks):
        both(p, finish)


def on_device(n_sky, n_exp, sky_model, eigen_weights, exposures, row_taps, col_taps, offsets, valid_blocks):
    count, rows, cols = eigen_weights.shape
    frames = exposures.shape[0]
    tall = rows + 2 * SLOT
    chunks = cols // CHUNK
    piece = cols // n_exp
    vmem = pl.BlockSpec(memory_space=pltpu.VMEM)
    edge = (chunks, frames * 2 * REACH, CHUNK + LANE)
    return pl.pallas_call(
        functools.partial(main_kernel, n_sky, n_exp),
        in_specs=[pl.BlockSpec(memory_space=pl.ANY)] * 7,
        out_specs=vmem,
        out_shape=pltpu.VMEM((rows, piece), F32),
        scratch_shapes=[
            pltpu.SMEM(offsets.shape, jnp.int32),
            pltpu.SMEM(valid_blocks.shape, jnp.int32),
            pltpu.VMEM(row_taps.shape, BF16),
            pltpu.VMEM(col_taps.shape, BF16),
            pltpu.VMEM((rows, cols), BF16),
            pltpu.VMEM((count, rows, cols), BF16),
            pltpu.VMEM((frames, rows, cols), BF16),
            pltpu.VMEM((count, 256, frames * LANE), BF16),
            pltpu.VMEM((count, frames * LANE, 256), BF16),
            pltpu.VMEM((frames, tall, count * rows), BF16),
            pltpu.VMEM((frames, count * rows, LANE), BF16),
            pltpu.VMEM((frames, rows, LANE), F32),
            pltpu.VMEM((frames, 8, cols + LANE), F32),
            pltpu.VMEM((count, rows, cols + 2 * LANE), BF16),
            pltpu.VMEM((frames, count * rows, CHUNK + LANE), BF16),
            pltpu.VMEM((frames, rows, cols + LANE), F32),
            pltpu.VMEM((frames, LANE, CHUNK + LANE), BF16),
            pltpu.VMEM((count, rows, (cols + LANE) * frames), BF16),
            pltpu.VMEM((rows, piece), F32),
            pltpu.VMEM((n_exp, rows, piece), BF16),
            pltpu.VMEM((n_exp, rows, piece), BF16),
        ]
        + [pltpu.VMEM(edge, BF16)] * 4
        + [pltpu.VMEM((frames * SLOT, LANE), BF16)] * 4
        + [pltpu.SemaphoreType.DMA((2, chunks))] * 2
        + [pltpu.SemaphoreType.DMA((2,))] * 2
        + [pltpu.SemaphoreType.DMA((n_exp,))] * 2
        + [pltpu.SemaphoreType.DMA((chunks + 6,))],
        compiler_params=pltpu.CompilerParams(
            collective_id=0, has_side_effects=True, vmem_limit_bytes=60 * 1024 * 1024
        ),
        name="gradient",
    )(offsets, valid_blocks, row_taps, col_taps, sky_model, eigen_weights, exposures)


def solution(mesh):
    return jax.shard_map(
        functools.partial(on_device, mesh.shape["sky"], mesh.shape["exp"]),
        mesh=mesh,
        in_specs=(
            P("sky", None),
            P(None, "sky", None),
            P("exp", "sky", None),
            P("exp", None, None),
            P("exp", None, None),
            P("exp"),
            P("exp", "sky"),
        ),
        out_specs=P("sky", "exp"),
        check_vma=False,
    )
```

```python
import functools

import jax
import jax.numpy as jnp
from jax import lax
from jax.experimental import pallas as pl
from jax.experimental.pallas import tpu as pltpu
from jax.sharding import PartitionSpec as P

F32 = jnp.float32
BF16 = jnp.bfloat16
LANE = 128
PAD = 64
SLOT = 24
REACH = 20
BEHIND = 3
DEPTH = 2
CHUNK = 512


def lagged(taps, lanes, sign, start):
    width = taps.shape[1]
    lane = lax.broadcasted_iota(jnp.int32, (width, lanes), 1)
    lag = jnp.where(lane < lanes // 2, lane, lane - lanes)
    tap = lax.broadcasted_iota(jnp.int32, (width, lanes), 0)
    onehot = jnp.where(tap == sign * lag + start, 1.0, 0.0).astype(BF16)
    return jnp.dot(taps, onehot, preferred_element_type=F32)


def toeplitz(row, height, shift=0):
    full = jnp.broadcast_to(row, (height, row.shape[1]))
    return pltpu.roll(full, shift, 1, stride=1, stride_axis=0)


def forward_tables(frames, count, offs, rt, ct, t1, ra):
    half = rt.shape[2] // 2
    rows = ra.shape[1] - 2 * SLOT
    lane = lax.broadcasted_iota(jnp.int32, (1, LANE), 1)
    for e in range(frames):
        rtaps = rt[e]
        ahead = lagged(ct[e], 256, -1, offs[e] + half - PAD)
        own = lagged(rtaps, LANE, 1, half)
        up = lagged(rtaps, LANE, 1, SLOT + half)
        down = lagged(rtaps, LANE, 1, half - rows)
        pair = []
        for k in range(count):
            one = slice(k, k + 1)
            band = toeplitz(ahead[one], LANE)
            at = slice(e * LANE, (e + 1) * LANE)
            t1[k, :LANE, at] = band[:, :LANE].astype(BF16)
            t1[k, LANE:, at] = band[:, LANE:].astype(BF16)
            side = (k % 2) * 64
            pair.append(
                jnp.concatenate(
                    [
                        toeplitz(own[one], rows, side),
                        toeplitz(up[one], SLOT, side),
                        toeplitz(down[one], SLOT, side),
                    ],
                    axis=0,
                )
            )
            if k % 2:
                both = jnp.where(lane < 64, pair[0], pair[1])
                ra[e, :, (k // 2) * LANE : (k // 2 + 1) * LANE] = both.astype(BF16)
                pair = []


def backward_tables(frames, count, rows, offs, rt, ct, t2, rb):
    half = rt.shape[2] // 2
    lane = lax.broadcasted_iota(jnp.int32, (1, LANE), 1)
    for e in range(frames):
        rtaps = rt[e]
        back = lagged(ct[e], 256, 1, offs[e] + half - PAD)
        own = lagged(rtaps, LANE, -1, half)
        above = lagged(rtaps, LANE, -1, SLOT + half)
        below = lagged(rtaps, LANE, -1, half - rows)
        for k in range(count):
            one = slice(k, k + 1)
            t2[k, e * LANE : (e + 1) * LANE, :] = toeplitz(back[one], LANE).astype(BF16)
            a = toeplitz(own[one], rows)
            b = toeplitz(above[one], rows, rows)
            c = toeplitz(below[one], rows, rows + SLOT)
            table = jnp.where(
                lane < rows,
                a,
                jnp.where(lane < rows + SLOT, b, jnp.where(lane < rows + 2 * SLOT, c, 0.0)),
            )
            rb[e, k * rows : (k + 1) * rows, :] = table.astype(BF16)


def mask_tables(cols, offs, valid, rowm, colm, mup_out, mdown_out):
    frames, rows = rowm.shape[:2]
    nblock = valid.shape[1]
    ups, downs = [], []
    for e in range(frames):
        row = lax.broadcasted_iota(jnp.int32, (rows, LANE), 0)
        block = row // (rows // nblock)
        mask = jnp.zeros((rows, LANE), F32)
        for b in range(nblock):
            mask = jnp.where(block == b, valid[e, b].astype(F32), mask)
        rowm[e] = mask
        ups.append(jnp.where(row < REACH, mask, 0.0)[:SLOT])
        downs.append(jnp.where(row >= rows - REACH, mask, 0.0)[rows - SLOT :])
        col = lax.broadcasted_iota(jnp.int32, (8, cols + LANE), 1) - PAD
        low = jnp.maximum(offs[e], 0)
        high = cols + jnp.minimum(offs[e], 0)
        colm[e] = jnp.where((col >= low) & (col < high), 1.0, 0.0)
    mup_out[...] = jnp.concatenate(ups, axis=0).astype(BF16)
    mdown_out[...] = jnp.concatenate(downs, axis=0).astype(BF16)


def main_kernel(
    n_sky, n_exp, offs_hbm, valid_hbm, rt_hbm, ct_hbm, sky_hbm, w_hbm, ex_hbm, out,
    offs, valid, rt, ct,
    sky, w, ex, t1, t2, ra, rb, rowm, colm, prod, blur, img, res, lift, own, grads, landed,
    up_out, down_out, up_in, down_in, mup_out, mdown_out, mup_in, mdown_in,
    s_send, s_recv, m_send, m_recv, g_send, g_recv, loads,
):
    count, rows, cols = w.shape
    frames = ex.shape[0]
    tall = rows + 2 * SLOT
    chunks = cols // CHUNK
    piece = cols // n_exp
    per = CHUNK // piece
    z = lax.axis_index("sky")
    me = lax.axis_index("exp")
    has_up = z > 0
    has_down = z < n_sky - 1
    chip = me // 2
    rising = lax.rem(chip, 2)
    base = 2 * chip + rising if per == 1 else me // per
    far = (me != base) & (per == 1)

    def walk(p):
        return lax.rem(base + (2 * rising - 1) * (1 + p) + 2 * chunks, chunks)

    def order(p):
        return walk(jnp.where(far & (p >= chunks - 2), 2 * chunks - 3 - p, p))

    def chunk(i):
        return pl.ds(pl.multiple_of(i * CHUNK, CHUNK), CHUNK)

    def load_w(i):
        at = chunk(i)
        return pltpu.make_async_copy(w_hbm.at[:, :, at], w.at[:, :, at], loads.at[i])

    load_sky = pltpu.make_async_copy(sky_hbm, sky, loads.at[chunks])
    load_ex = pltpu.make_async_copy(ex_hbm, ex, loads.at[chunks + 1])
    barrier = pltpu.get_barrier_semaphore()

    for step in range(1, n_exp):
        pl.semaphore_signal(barrier, inc=1, device_id={"exp": lax.rem(me + step, n_exp)})

    @pl.when(has_up)
    def _():
        pl.semaphore_signal(barrier, inc=1, device_id={"sky": z - 1})

    @pl.when(has_down)
    def _():
        pl.semaphore_signal(barrier, inc=1, device_id={"sky": z + 1})

    small = [
        pltpu.make_async_copy(src, dst, loads.at[chunks + 2 + n])
        for n, (src, dst) in enumerate(
            [(offs_hbm, offs), (rt_hbm, rt), (ct_hbm, ct), (valid_hbm, valid)]
        )
    ]
    for copy in small:
        copy.start()
    load_sky.start()
    load_w(walk(chunks - 1)).start()
    load_w(walk(0)).start()
    load_w(walk(1)).start()
    load_ex.start()
    for p in range(2, chunks - 1):
        load_w(walk(p)).start()

    @pl.when(jnp.logical_not(has_up))
    def _():
        down_in[...] = jnp.zeros(down_in.shape, BF16)
        mdown_in[...] = jnp.zeros(mdown_in.shape, BF16)

    @pl.when(jnp.logical_not(has_down))
    def _():
        up_in[...] = jnp.zeros(up_in.shape, BF16)
        mup_in[...] = jnp.zeros(mup_in.shape, BF16)

    for e in range(frames):
        res[e, tall:, :] = jnp.zeros((LANE - tall, CHUNK + LANE), BF16)

    prod[:, :, :LANE] = jnp.zeros((count, rows, LANE), BF16)
    prod[:, :, cols + LANE :] = jnp.zeros((count, rows, LANE), BF16)

    def multiply(i):
        load_w(i).wait()
        at = chunk(i)
        to = pl.ds(pl.multiple_of(i * CHUNK + LANE, LANE), CHUNK)
        model = sky[:, at]
        for k in range(count):
            prod[k, :, to] = w[k, :, at] * model

    def near(begin):
        return pl.ds(pl.multiple_of(begin, LANE), LANE)

    def lanes_of(i, blocks):
        swapped = far & (i == order(chunks - 2))
        side = jnp.where(swapped, 1 - rising, rising)
        start = i * CHUNK + {3: LANE, 4: side * LANE, 5: 0}[blocks]
        return start, pl.ds(pl.multiple_of(start, LANE), blocks * LANE)

    def edge_copies(i, blocks):
        size = pl.ds(0, blocks * LANE)
        up = pltpu.make_async_remote_copy(
            src_ref=up_out.at[i, :, size], dst_ref=up_in.at[i, :, size],
            send_sem=s_send.at[0, i], recv_sem=s_recv.at[0, i], device_id={"sky": z - 1},
        )
        down = pltpu.make_async_remote_copy(
            src_ref=down_out.at[i, :, size], dst_ref=down_in.at[i, :, size],
            send_sem=s_send.at[1, i], recv_sem=s_recv.at[1, i], device_id={"sky": z + 1},
        )
        return up, down

    def mask_copies():
        up = pltpu.make_async_remote_copy(
            src_ref=mup_out, dst_ref=mup_in,
            send_sem=m_send.at[0], recv_sem=m_recv.at[0], device_id={"sky": z - 1},
        )
        down = pltpu.make_async_remote_copy(
            src_ref=mdown_out, dst_ref=mdown_in,
            send_sem=m_send.at[1], recv_sem=m_recv.at[1], device_id={"sky": z + 1},
        )
        return up, down

    def start(pair):
        @pl.when(has_up)
        def _():
            pair[0].start()

        @pl.when(has_down)
        def _():
            pair[1].start()

    def arrive(pair):
        @pl.when(has_down)
        def _():
            pair[0].wait_recv()

        @pl.when(has_up)
        def _():
            pair[1].wait_recv()

    def drain(pair):
        @pl.when(has_up)
        def _():
            pair[0].wait_send()

        @pl.when(has_down)
        def _():
            pair[1].wait_send()

    def row_of(width):
        return lax.broadcasted_iota(jnp.int32, (SLOT, width), 0)

    def forward(i, blocks):
        begin, lanes = lanes_of(i, blocks)
        width = blocks * LANE
        for k in range(count):
            left = jnp.concatenate(
                [
                    prod[k, :, pl.ds(pl.multiple_of(begin + j * LANE, LANE), 256)]
                    for j in range(blocks)
                ],
                axis=0,
            )
            got = jnp.dot(left, t1[k], preferred_element_type=F32).astype(BF16)
            for e in range(frames):
                for j in range(blocks):
                    blur[e, k * rows : (k + 1) * rows, j * LANE : (j + 1) * LANE] = got[
                        j * rows : (j + 1) * rows, e * LANE : (e + 1) * LANE
                    ]
        row = row_of(width)
        ups, downs = [], []
        for e in range(frames):
            image = jnp.dot(ra[e], blur[e, :, :width], preferred_element_type=F32)
            parts = [
                ex[e, :, near(jnp.clip(begin + (j - 1) * LANE, 0, cols - LANE))]
                for j in range(blocks + 1)
            ]
            seen = jnp.concatenate(parts, axis=1)[:, PAD : PAD + width]
            value = image[:rows] - seen.astype(F32)
            img[e, :, lanes] = value
            up = image[rows : rows + SLOT]
            down = image[rows + SLOT :]
            head = jnp.where(row < REACH, value[:SLOT], 0.0)
            tail = jnp.where(row >= SLOT - REACH, value[rows - SLOT :], 0.0)
            ups += [head[:16], head[16:] + up[:8], up[8:]]
            downs += [down[:16], down[16:] + tail[:8], tail[8:]]
        up_out[i, :, :width] = jnp.concatenate(ups, axis=0).astype(BF16)
        down_out[i, :, :width] = jnp.concatenate(downs, axis=0).astype(BF16)

    def remain(i, blocks):
        begin, lanes = lanes_of(i, blocks)
        width = blocks * LANE
        arrive(edge_copies(i, blocks))
        above = down_in[i, :, :width].astype(F32)
        below = up_in[i, :, :width].astype(F32)
        mine_up = up_out[i, :, :width].astype(F32)
        mine_down = down_out[i, :, :width].astype(F32)
        mask_up = mdown_in[...].astype(F32)
        mask_down = mup_in[...].astype(F32)
        row = row_of(width)
        for e in range(frames):
            base = e * 2 * REACH
            image = img[e, :, lanes]
            slot = slice(e * SLOT, (e + 1) * SLOT)
            low = slice(base, base + SLOT)
            high = slice(base + 16, base + 16 + SLOT)
            value = jnp.concatenate(
                [
                    image[:SLOT] + jnp.where(row < REACH, above[low], 0.0),
                    image[SLOT : rows - SLOT],
                    image[rows - SLOT :] + jnp.where(row >= SLOT - REACH, below[high], 0.0),
                    above[high] + mine_up[high],
                    below[low] + mine_down[low],
                ],
                axis=0,
            )
            mask = jnp.concatenate([rowm[e], mask_up[slot], mask_down[slot]], axis=0)
            value = value * colm[e, :1, lanes] * jnp.tile(mask, (1, blocks))
            res[e, :tall, :width] = value.astype(BF16)
            got = jnp.dot(rb[e], res[e, :, :width], preferred_element_type=F32).astype(BF16)
            for k in range(count):
                for j in range(blocks):
                    to = pl.ds(pl.multiple_of((begin + j * LANE) * frames + e * LANE, LANE), LANE)
                    lift[k, :, to] = got[k * rows : (k + 1) * rows, j * LANE : (j + 1) * LANE]

    def backward(i):
        at = chunk(i)
        total = None
        for k in range(count):
            left = jnp.concatenate(
                [
                    lift[k, :, pl.ds(pl.multiple_of((i * CHUNK + j * LANE) * frames, LANE), frames * LANE)]
                    for j in range(CHUNK // LANE + 1)
                ],
                axis=0,
            )
            got = jnp.dot(left, t2[k], preferred_element_type=F32)
            lifted = jnp.concatenate(
                [
                    got[j * rows : (j + 1) * rows, LANE:] + got[(j + 1) * rows : (j + 2) * rows, :LANE]
                    for j in range(CHUNK // LANE)
                ],
                axis=1,
            )
            term = w[k, :, at].astype(F32) * lifted
            total = term if total is None else total + term
        for part in range(per):
            to = i * per + part
            value = total[:, part * piece : (part + 1) * piece]

            @pl.when(to == me)
            def _(value=value):
                own[...] = value

            @pl.when(to != me)
            def _(value=value, to=to):
                grads[to] = value.astype(BF16)
                gradient_copy(to).start()

    def gradient_copy(to):
        return pltpu.make_async_remote_copy(
            src_ref=grads.at[to], dst_ref=landed.at[me],
            send_sem=g_send.at[to], recv_sem=g_recv.at[me], device_id={"exp": to},
        )

    def collect(begin, end):
        for q in range(begin, end):
            step = n_exp // 2 - 1 - q // 2
            there = lax.rem(chip + (1 - 2 * rising) * step + n_exp // 2, n_exp // 2)
            src = 2 * there + q % 2 if step else me + 1 - 2 * lax.rem(me, 2)
            pltpu.make_async_remote_copy(
                src_ref=grads.at[src], dst_ref=landed.at[src],
                send_sem=g_send.at[src], recv_sem=g_recv.at[src], device_id={"exp": src},
            ).wait_recv()
            piece_sum = landed[src].astype(F32)
            out[...] = piece_sum if q == 0 else out[...] + piece_sum

    early = n_exp - 4 if per == 1 else 0

    def both(p, stage):
        i = order(p)
        edge = (1 - rising) * (chunks - 1)
        wraps = order(0) == edge
        wide = (i == edge) | (p == 0) | (far & wraps & (p == chunks - 2))
        narrow = (p == chunks - 1) & (i != edge) & (far | jnp.logical_not(wraps))

        @pl.when(wide)
        def _():
            stage(i, 5)

        @pl.when(jnp.logical_not(wide | narrow))
        def _():
            stage(i, 4)

        @pl.when(narrow)
        def _():
            stage(i, 3)

    def send(i, blocks):
        start(edge_copies(i, blocks))

    def finish(i, blocks):
        drain(edge_copies(i, blocks))

    for copy in small:
        copy.wait()
    forward_tables(frames, count, offs, rt, ct, t1, ra)
    mask_tables(cols, offs, valid, rowm, colm, mup_out, mdown_out)
    load_sky.wait()
    multiply(walk(chunks - 1))
    multiply(walk(0))
    load_ex.wait()

    @pl.loop(0, chunks + BEHIND)
    def _(p):
        @pl.when(p < chunks - 2)
        def _():
            multiply(walk(p + 1))

        @pl.when(p < chunks)
        def _():
            both(p, forward)

        @pl.when(p == 0)
        def _():
            neighbours = (z + n_sky - 1) // n_sky + (2 * n_sky - 2 - z) // n_sky
            pl.semaphore_wait(barrier, n_exp - 1 + neighbours)

        @pl.when((p >= DEPTH) & (p < chunks))
        def _():
            both(p - DEPTH, finish)

        @pl.when(p < chunks)
        def _():
            both(p, send)

        @pl.when(p == 0)
        def _():
            start(mask_copies())
            backward_tables(frames, count, rows, offs, rt, ct, t2, rb)

        @pl.when(p == BEHIND)
        def _():
            arrive(mask_copies())

        @pl.when(p == chunks + BEHIND - 1)
        def _():
            collect(0, early)

        @pl.when(p >= BEHIND)
        def _():
            both(p - BEHIND, remain)
            backward(order(p - BEHIND))

    collect(early, n_exp - 1)
    out[...] = out[...] + own[...]
    for step in range(1, n_exp):
        gradient_copy(lax.rem(me + step, n_exp)).wait_send()
    drain(mask_copies())

    for p in range(chunks - DEPTH, chunks):
        both(p, finish)


def on_device(n_sky, n_exp, sky_model, eigen_weights, exposures, row_taps, col_taps, offsets, valid_blocks):
    count, rows, cols = eigen_weights.shape
    frames = exposures.shape[0]
    tall = rows + 2 * SLOT
    chunks = cols // CHUNK
    piece = cols // n_exp
    vmem = pl.BlockSpec(memory_space=pltpu.VMEM)
    edge = (chunks, frames * 2 * REACH, CHUNK + LANE)
    return pl.pallas_call(
        functools.partial(main_kernel, n_sky, n_exp),
        in_specs=[pl.BlockSpec(memory_space=pl.ANY)] * 7,
        out_specs=vmem,
        out_shape=pltpu.VMEM((rows, piece), F32),
        scratch_shapes=[
            pltpu.SMEM(offsets.shape, jnp.int32),
            pltpu.SMEM(valid_blocks.shape, jnp.int32),
            pltpu.VMEM(row_taps.shape, BF16),
            pltpu.VMEM(col_taps.shape, BF16),
            pltpu.VMEM((rows, cols), BF16),
            pltpu.VMEM((count, rows, cols), BF16),
            pltpu.VMEM((frames, rows, cols), BF16),
            pltpu.VMEM((count, 256, frames * LANE), BF16),
            pltpu.VMEM((count, frames * LANE, 256), BF16),
            pltpu.VMEM((frames, tall, count * rows), BF16),
            pltpu.VMEM((frames, count * rows, LANE), BF16),
            pltpu.VMEM((frames, rows, LANE), F32),
            pltpu.VMEM((frames, 8, cols + LANE), F32),
            pltpu.VMEM((count, rows, cols + 2 * LANE), BF16),
            pltpu.VMEM((frames, count * rows, CHUNK + LANE), BF16),
            pltpu.VMEM((frames, rows, cols + LANE), F32),
            pltpu.VMEM((frames, LANE, CHUNK + LANE), BF16),
            pltpu.VMEM((count, rows, (cols + LANE) * frames), BF16),
            pltpu.VMEM((rows, piece), F32),
            pltpu.VMEM((n_exp, rows, piece), BF16),
            pltpu.VMEM((n_exp, rows, piece), BF16),
        ]
        + [pltpu.VMEM(edge, BF16)] * 4
        + [pltpu.VMEM((frames * SLOT, LANE), BF16)] * 4
        + [pltpu.SemaphoreType.DMA((2, chunks))] * 2
        + [pltpu.SemaphoreType.DMA((2,))] * 2
        + [pltpu.SemaphoreType.DMA((n_exp,))] * 2
        + [pltpu.SemaphoreType.DMA((chunks + 6,))],
        compiler_params=pltpu.CompilerParams(
            collective_id=0, has_side_effects=True, vmem_limit_bytes=60 * 1024 * 1024
        ),
        name="gradient",
    )(offsets, valid_blocks, row_taps, col_taps, sky_model, eigen_weights, exposures)


def solution(mesh):
    return jax.shard_map(
        functools.partial(on_device, mesh.shape["sky"], mesh.shape["exp"]),
        mesh=mesh,
        in_specs=(
            P("sky", None),
            P(None, "sky", None),
            P("exp", "sky", None),
            P("exp", None, None),
            P("exp", None, None),
            P("exp"),
            P("exp", "sky"),
        ),
        out_specs=P("sky", "exp"),
        check_vma=False,
    )
```

```python
import functools

import jax
import jax.numpy as jnp
from jax import lax
from jax.experimental import pallas as pl
from jax.experimental.pallas import tpu as pltpu
from jax.sharding import PartitionSpec as P

F32 = jnp.float32
BF16 = jnp.bfloat16
LANE = 128
PAD = 64
SLOT = 24
REACH = 20
BEHIND = 3
DEPTH = 2
CHUNK = 512


def lagged(taps, lanes, sign, start):
    width = taps.shape[1]
    lane = lax.broadcasted_iota(jnp.int32, (width, lanes), 1)
    lag = jnp.where(lane < lanes // 2, lane, lane - lanes)
    tap = lax.broadcasted_iota(jnp.int32, (width, lanes), 0)
    onehot = jnp.where(tap == sign * lag + start, 1.0, 0.0).astype(BF16)
    return jnp.dot(taps, onehot, preferred_element_type=F32)


def toeplitz(row, height, shift=0):
    full = jnp.broadcast_to(row, (height, row.shape[1]))
    return pltpu.roll(full, shift, 1, stride=1, stride_axis=0)


def forward_tables(frames, count, offs, rt, ct, t1, ra):
    half = rt.shape[2] // 2
    rows = ra.shape[1] - 2 * SLOT
    lane = lax.broadcasted_iota(jnp.int32, (1, LANE), 1)
    for e in range(frames):
        rtaps = rt[e]
        ahead = lagged(ct[e], 256, -1, offs[e] + half - PAD)
        own = lagged(rtaps, LANE, 1, half)
        up = lagged(rtaps, LANE, 1, SLOT + half)
        down = lagged(rtaps, LANE, 1, half - rows)
        pair = []
        for k in range(count):
            one = slice(k, k + 1)
            band = toeplitz(ahead[one], LANE)
            at = slice(e * LANE, (e + 1) * LANE)
            t1[k, :LANE, at] = band[:, :LANE].astype(BF16)
            t1[k, LANE:, at] = band[:, LANE:].astype(BF16)
            side = (k % 2) * 64
            pair.append(
                jnp.concatenate(
                    [
                        toeplitz(own[one], rows, side),
                        toeplitz(up[one], SLOT, side),
                        toeplitz(down[one], SLOT, side),
                    ],
                    axis=0,
                )
            )
            if k % 2:
                both = jnp.where(lane < 64, pair[0], pair[1])
                ra[e, :, (k // 2) * LANE : (k // 2 + 1) * LANE] = both.astype(BF16)
                pair = []


def backward_tables(frames, count, rows, offs, rt, ct, t2, rb):
    half = rt.shape[2] // 2
    lane = lax.broadcasted_iota(jnp.int32, (1, LANE), 1)
    for e in range(frames):
        rtaps = rt[e]
        back = lagged(ct[e], 256, 1, offs[e] + half - PAD)
        own = lagged(rtaps, LANE, -1, half)
        above = lagged(rtaps, LANE, -1, SLOT + half)
        below = lagged(rtaps, LANE, -1, half - rows)
        for k in range(count):
            one = slice(k, k + 1)
            t2[k, e * LANE : (e + 1) * LANE, :] = toeplitz(back[one], LANE).astype(BF16)
            a = toeplitz(own[one], rows)
            b = toeplitz(above[one], rows, rows)
            c = toeplitz(below[one], rows, rows + SLOT)
            table = jnp.where(
                lane < rows,
                a,
                jnp.where(lane < rows + SLOT, b, jnp.where(lane < rows + 2 * SLOT, c, 0.0)),
            )
            rb[e, k * rows : (k + 1) * rows, :] = table.astype(BF16)


def mask_tables(cols, offs, valid, rowm, colm, mup_out, mdown_out):
    frames, rows = rowm.shape[:2]
    nblock = valid.shape[1]
    ups, downs = [], []
    for e in range(frames):
        row = lax.broadcasted_iota(jnp.int32, (rows, LANE), 0)
        block = row // (rows // nblock)
        mask = jnp.zeros((rows, LANE), F32)
        for b in range(nblock):
            mask = jnp.where(block == b, valid[e, b].astype(F32), mask)
        rowm[e] = mask
        ups.append(jnp.where(row < REACH, mask, 0.0)[:SLOT])
        downs.append(jnp.where(row >= rows - REACH, mask, 0.0)[rows - SLOT :])
        col = lax.broadcasted_iota(jnp.int32, (8, cols + LANE), 1) - PAD
        low = jnp.maximum(offs[e], 0)
        high = cols + jnp.minimum(offs[e], 0)
        colm[e] = jnp.where((col >= low) & (col < high), 1.0, 0.0)
    mup_out[...] = jnp.concatenate(ups, axis=0).astype(BF16)
    mdown_out[...] = jnp.concatenate(downs, axis=0).astype(BF16)


def main_kernel(
    n_sky, n_exp, offs_hbm, valid_hbm, rt_hbm, ct_hbm, sky_hbm, w_hbm, ex_hbm, out,
    offs, valid, rt, ct,
    sky, w, ex, t1, t2, ra, rb, rowm, colm, prod, blur, img, res, lift, own, grads, landed,
    up_out, down_out, up_in, down_in, mup_out, mdown_out, mup_in, mdown_in,
    s_send, s_recv, m_send, m_recv, g_send, g_recv, loads, ready,
):
    count, rows, cols = w.shape
    frames = ex.shape[0]
    tall = rows + 2 * SLOT
    chunks = cols // CHUNK
    piece = cols // n_exp
    per = CHUNK // piece
    z = lax.axis_index("sky")
    me = lax.axis_index("exp")
    has_up = z > 0
    has_down = z < n_sky - 1
    chip = me // 2
    rising = lax.rem(chip, 2)
    base = 2 * chip + rising if per == 1 else me // per
    far = (me != base) & (per == 1)

    def walk(p):
        return lax.rem(base + (2 * rising - 1) * (1 + p) + 2 * chunks, chunks)

    def order(p):
        return walk(jnp.where(far & (p >= chunks - 2), 2 * chunks - 3 - p, p))

    def chunk(i):
        return pl.ds(pl.multiple_of(i * CHUNK, CHUNK), CHUNK)

    def load_w(i):
        at = chunk(i)
        return pltpu.make_async_copy(w_hbm.at[:, :, at], w.at[:, :, at], loads.at[i])

    load_sky = pltpu.make_async_copy(sky_hbm, sky, loads.at[chunks])
    load_ex = pltpu.make_async_copy(ex_hbm, ex, loads.at[chunks + 1])
    barrier = pltpu.get_barrier_semaphore()

    across = n_exp // 2 - 1 - chip
    for step in range(1, n_exp):
        peer = lax.rem(me + step, n_exp)

        @pl.when(peer // 2 != across)
        def _(peer=peer):
            pl.semaphore_signal(barrier, inc=1, device_id={"exp": peer})

    @pl.when(has_up)
    def _():
        pl.semaphore_signal(barrier, inc=1, device_id={"sky": z - 1})

    @pl.when(has_down)
    def _():
        pl.semaphore_signal(barrier, inc=1, device_id={"sky": z + 1})

    small = [
        pltpu.make_async_copy(src, dst, loads.at[chunks + 2 + n])
        for n, (src, dst) in enumerate(
            [(offs_hbm, offs), (rt_hbm, rt), (ct_hbm, ct), (valid_hbm, valid)]
        )
    ]
    for copy in small:
        copy.start()
    load_sky.start()
    load_w(walk(chunks - 1)).start()
    load_w(walk(0)).start()
    load_w(walk(1)).start()
    load_ex.start()
    for p in range(2, chunks - 1):
        load_w(walk(p)).start()

    @pl.when(jnp.logical_not(has_up))
    def _():
        down_in[...] = jnp.zeros(down_in.shape, BF16)
        mdown_in[...] = jnp.zeros(mdown_in.shape, BF16)

    @pl.when(jnp.logical_not(has_down))
    def _():
        up_in[...] = jnp.zeros(up_in.shape, BF16)
        mup_in[...] = jnp.zeros(mup_in.shape, BF16)

    for e in range(frames):
        res[e, tall:, :] = jnp.zeros((LANE - tall, CHUNK + LANE), BF16)

    prod[:, :, :LANE] = jnp.zeros((count, rows, LANE), BF16)
    prod[:, :, cols + LANE :] = jnp.zeros((count, rows, LANE), BF16)

    def multiply(i):
        load_w(i).wait()
        at = chunk(i)
        to = pl.ds(pl.multiple_of(i * CHUNK + LANE, LANE), CHUNK)
        model = sky[:, at]
        for k in range(count):
            prod[k, :, to] = w[k, :, at] * model

    def near(begin):
        return pl.ds(pl.multiple_of(begin, LANE), LANE)

    def lanes_of(i, blocks):
        swapped = far & (i == order(chunks - 2))
        side = jnp.where(swapped, 1 - rising, rising)
        start = i * CHUNK + {3: LANE, 4: side * LANE, 5: 0}[blocks]
        return start, pl.ds(pl.multiple_of(start, LANE), blocks * LANE)

    def edge_copies(i, blocks):
        size = pl.ds(0, blocks * LANE)
        up = pltpu.make_async_remote_copy(
            src_ref=up_out.at[i, :, size], dst_ref=up_in.at[i, :, size],
            send_sem=s_send.at[0, i], recv_sem=s_recv.at[0, i], device_id={"sky": z - 1},
        )
        down = pltpu.make_async_remote_copy(
            src_ref=down_out.at[i, :, size], dst_ref=down_in.at[i, :, size],
            send_sem=s_send.at[1, i], recv_sem=s_recv.at[1, i], device_id={"sky": z + 1},
        )
        return up, down

    def mask_copies():
        up = pltpu.make_async_remote_copy(
            src_ref=mup_out, dst_ref=mup_in,
            send_sem=m_send.at[0], recv_sem=m_recv.at[0], device_id={"sky": z - 1},
        )
        down = pltpu.make_async_remote_copy(
            src_ref=mdown_out, dst_ref=mdown_in,
            send_sem=m_send.at[1], recv_sem=m_recv.at[1], device_id={"sky": z + 1},
        )
        return up, down

    def start(pair):
        @pl.when(has_up)
        def _():
            pair[0].start()

        @pl.when(has_down)
        def _():
            pair[1].start()

    def arrive(pair):
        @pl.when(has_down)
        def _():
            pair[0].wait_recv()

        @pl.when(has_up)
        def _():
            pair[1].wait_recv()

    def drain(pair):
        @pl.when(has_up)
        def _():
            pair[0].wait_send()

        @pl.when(has_down)
        def _():
            pair[1].wait_send()

    def row_of(width):
        return lax.broadcasted_iota(jnp.int32, (SLOT, width), 0)

    def forward(i, blocks):
        begin, lanes = lanes_of(i, blocks)
        width = blocks * LANE
        for k in range(count):
            left = jnp.concatenate(
                [
                    prod[k, :, pl.ds(pl.multiple_of(begin + j * LANE, LANE), 256)]
                    for j in range(blocks)
                ],
                axis=0,
            )
            got = jnp.dot(left, t1[k], preferred_element_type=F32).astype(BF16)
            for e in range(frames):
                for j in range(blocks):
                    blur[e, k * rows : (k + 1) * rows, j * LANE : (j + 1) * LANE] = got[
                        j * rows : (j + 1) * rows, e * LANE : (e + 1) * LANE
                    ]
        row = row_of(width)
        ups, downs = [], []
        for e in range(frames):
            image = jnp.dot(ra[e], blur[e, :, :width], preferred_element_type=F32)
            parts = [
                ex[e, :, near(jnp.clip(begin + (j - 1) * LANE, 0, cols - LANE))]
                for j in range(blocks + 1)
            ]
            seen = jnp.concatenate(parts, axis=1)[:, PAD : PAD + width]
            value = image[:rows] - seen.astype(F32)
            img[e, :, lanes] = value
            up = image[rows : rows + SLOT]
            down = image[rows + SLOT :]
            head = jnp.where(row < REACH, value[:SLOT], 0.0)
            tail = jnp.where(row >= SLOT - REACH, value[rows - SLOT :], 0.0)
            ups += [head[:16], head[16:] + up[:8], up[8:]]
            downs += [down[:16], down[16:] + tail[:8], tail[8:]]
        up_out[i, :, :width] = jnp.concatenate(ups, axis=0).astype(BF16)
        down_out[i, :, :width] = jnp.concatenate(downs, axis=0).astype(BF16)

    def remain(i, blocks):
        begin, lanes = lanes_of(i, blocks)
        width = blocks * LANE
        arrive(edge_copies(i, blocks))
        above = down_in[i, :, :width].astype(F32)
        below = up_in[i, :, :width].astype(F32)
        mine_up = up_out[i, :, :width].astype(F32)
        mine_down = down_out[i, :, :width].astype(F32)
        mask_up = mdown_in[...].astype(F32)
        mask_down = mup_in[...].astype(F32)
        row = row_of(width)
        for e in range(frames):
            base = e * 2 * REACH
            image = img[e, :, lanes]
            slot = slice(e * SLOT, (e + 1) * SLOT)
            low = slice(base, base + SLOT)
            high = slice(base + 16, base + 16 + SLOT)
            value = jnp.concatenate(
                [
                    image[:SLOT] + jnp.where(row < REACH, above[low], 0.0),
                    image[SLOT : rows - SLOT],
                    image[rows - SLOT :] + jnp.where(row >= SLOT - REACH, below[high], 0.0),
                    above[high] + mine_up[high],
                    below[low] + mine_down[low],
                ],
                axis=0,
            )
            mask = jnp.concatenate([rowm[e], mask_up[slot], mask_down[slot]], axis=0)
            value = value * colm[e, :1, lanes] * jnp.tile(mask, (1, blocks))
            res[e, :tall, :width] = value.astype(BF16)
            got = jnp.dot(rb[e], res[e, :, :width], preferred_element_type=F32).astype(BF16)
            for k in range(count):
                for j in range(blocks):
                    to = pl.ds(pl.multiple_of((begin + j * LANE) * frames + e * LANE, LANE), LANE)
                    lift[k, :, to] = got[k * rows : (k + 1) * rows, j * LANE : (j + 1) * LANE]

    def backward(i):
        at = chunk(i)
        total = None
        for k in range(count):
            left = jnp.concatenate(
                [
                    lift[k, :, pl.ds(pl.multiple_of((i * CHUNK + j * LANE) * frames, LANE), frames * LANE)]
                    for j in range(CHUNK // LANE + 1)
                ],
                axis=0,
            )
            got = jnp.dot(left, t2[k], preferred_element_type=F32)
            lifted = jnp.concatenate(
                [
                    got[j * rows : (j + 1) * rows, LANE:] + got[(j + 1) * rows : (j + 2) * rows, :LANE]
                    for j in range(CHUNK // LANE)
                ],
                axis=1,
            )
            term = w[k, :, at].astype(F32) * lifted
            total = term if total is None else total + term
        for part in range(per):
            to = i * per + part
            value = total[:, part * piece : (part + 1) * piece]

            @pl.when(to == me)
            def _(value=value):
                own[...] = value

            @pl.when(to != me)
            def _(value=value, to=to):
                grads[to] = value.astype(BF16)
                gradient_copy(to).start()

    def gradient_copy(to):
        return pltpu.make_async_remote_copy(
            src_ref=grads.at[to], dst_ref=landed.at[me],
            send_sem=g_send.at[to], recv_sem=g_recv.at[me], device_id={"exp": to},
        )

    def collect(begin, end):
        for q in range(begin, end):
            step = n_exp // 2 - 1 - q // 2
            there = lax.rem(chip + (1 - 2 * rising) * step + n_exp // 2, n_exp // 2)
            src = 2 * there + q % 2 if step else me + 1 - 2 * lax.rem(me, 2)
            pltpu.make_async_remote_copy(
                src_ref=grads.at[src], dst_ref=landed.at[src],
                send_sem=g_send.at[src], recv_sem=g_recv.at[src], device_id={"exp": src},
            ).wait_recv()
            piece_sum = landed[src].astype(F32)
            out[...] = piece_sum if q == 0 else out[...] + piece_sum

    early = n_exp - 4 if per == 1 else 0

    def both(p, stage):
        i = order(p)
        edge = (1 - rising) * (chunks - 1)
        wraps = order(0) == edge
        wide = (i == edge) | (p == 0) | (far & wraps & (p == chunks - 2))
        narrow = (p == chunks - 1) & (i != edge) & (far | jnp.logical_not(wraps))

        @pl.when(wide)
        def _():
            stage(i, 5)

        @pl.when(jnp.logical_not(wide | narrow))
        def _():
            stage(i, 4)

        @pl.when(narrow)
        def _():
            stage(i, 3)

    def send(i, blocks):
        start(edge_copies(i, blocks))

    def finish(i, blocks):
        drain(edge_copies(i, blocks))

    for copy in small:
        copy.wait()
    forward_tables(frames, count, offs, rt, ct, t1, ra)
    mask_tables(cols, offs, valid, rowm, colm, mup_out, mdown_out)
    load_sky.wait()
    multiply(walk(chunks - 1))
    multiply(walk(0))
    load_ex.wait()

    @pl.loop(0, chunks + BEHIND)
    def _(p):
        @pl.when(p < chunks - 2)
        def _():
            multiply(walk(p + 1))

        @pl.when(p < chunks)
        def _():
            both(p, forward)

        @pl.when(p == 0)
        def _():
            neighbours = (z + n_sky - 1) // n_sky + (2 * n_sky - 2 - z) // n_sky
            pl.semaphore_wait(barrier, n_exp - 3 + neighbours)
            pl.semaphore_signal(ready, inc=1, device_id={"exp": me + 2 - 4 * rising})

        @pl.when((p >= DEPTH) & (p < chunks))
        def _():
            both(p - DEPTH, finish)

        @pl.when(p < chunks)
        def _():
            both(p, send)

        @pl.when(p == 0)
        def _():
            start(mask_copies())
            backward_tables(frames, count, rows, offs, rt, ct, t2, rb)

        @pl.when(p == BEHIND)
        def _():
            arrive(mask_copies())
            pl.semaphore_wait(ready, 1)

        @pl.when(p == chunks + BEHIND - 1)
        def _():
            collect(0, early)

        @pl.when(p >= BEHIND)
        def _():
            both(p - BEHIND, remain)
            backward(order(p - BEHIND))

    collect(early, n_exp - 1)
    out[...] = out[...] + own[...]
    for step in range(1, n_exp):
        gradient_copy(lax.rem(me + step, n_exp)).wait_send()
    drain(mask_copies())

    for p in range(chunks - DEPTH, chunks):
        both(p, finish)


def on_device(n_sky, n_exp, sky_model, eigen_weights, exposures, row_taps, col_taps, offsets, valid_blocks):
    count, rows, cols = eigen_weights.shape
    frames = exposures.shape[0]
    tall = rows + 2 * SLOT
    chunks = cols // CHUNK
    piece = cols // n_exp
    vmem = pl.BlockSpec(memory_space=pltpu.VMEM)
    edge = (chunks, frames * 2 * REACH, CHUNK + LANE)
    return pl.pallas_call(
        functools.partial(main_kernel, n_sky, n_exp),
        in_specs=[pl.BlockSpec(memory_space=pl.ANY)] * 7,
        out_specs=vmem,
        out_shape=pltpu.VMEM((rows, piece), F32),
        scratch_shapes=[
            pltpu.SMEM(offsets.shape, jnp.int32),
            pltpu.SMEM(valid_blocks.shape, jnp.int32),
            pltpu.VMEM(row_taps.shape, BF16),
            pltpu.VMEM(col_taps.shape, BF16),
            pltpu.VMEM((rows, cols), BF16),
            pltpu.VMEM((count, rows, cols), BF16),
            pltpu.VMEM((frames, rows, cols), BF16),
            pltpu.VMEM((count, 256, frames * LANE), BF16),
            pltpu.VMEM((count, frames * LANE, 256), BF16),
            pltpu.VMEM((frames, tall, count * rows), BF16),
            pltpu.VMEM((frames, count * rows, LANE), BF16),
            pltpu.VMEM((frames, rows, LANE), F32),
            pltpu.VMEM((frames, 8, cols + LANE), F32),
            pltpu.VMEM((count, rows, cols + 2 * LANE), BF16),
            pltpu.VMEM((frames, count * rows, CHUNK + LANE), BF16),
            pltpu.VMEM((frames, rows, cols + LANE), F32),
            pltpu.VMEM((frames, LANE, CHUNK + LANE), BF16),
            pltpu.VMEM((count, rows, (cols + LANE) * frames), BF16),
            pltpu.VMEM((rows, piece), F32),
            pltpu.VMEM((n_exp, rows, piece), BF16),
            pltpu.VMEM((n_exp, rows, piece), BF16),
        ]
        + [pltpu.VMEM(edge, BF16)] * 4
        + [pltpu.VMEM((frames * SLOT, LANE), BF16)] * 4
        + [pltpu.SemaphoreType.DMA((2, chunks))] * 2
        + [pltpu.SemaphoreType.DMA((2,))] * 2
        + [pltpu.SemaphoreType.DMA((n_exp,))] * 2
        + [pltpu.SemaphoreType.DMA((chunks + 6,)), pltpu.SemaphoreType.REGULAR],
        compiler_params=pltpu.CompilerParams(
            collective_id=0, has_side_effects=True, vmem_limit_bytes=60 * 1024 * 1024
        ),
        name="gradient",
    )(offsets, valid_blocks, row_taps, col_taps, sky_model, eigen_weights, exposures)


def solution(mesh):
    return jax.shard_map(
        functools.partial(on_device, mesh.shape["sky"], mesh.shape["exp"]),
        mesh=mesh,
        in_specs=(
            P("sky", None),
            P(None, "sky", None),
            P("exp", "sky", None),
            P("exp", None, None),
            P("exp", None, None),
            P("exp"),
            P("exp", "sky"),
        ),
        out_specs=P("sky", "exp"),
        check_vma=False,
    )
```
